256 devices in a mesh: seq: 16 (over x_hi, z), rep: 16 (over y, x_lo, core).
Axes of the slice: x: 4 (x_hi: 2, x_lo: 2; x = x_hi * 2 + x_lo), y: 4, z: 8, core: 2. Of those that a mesh axis runs over, the one named last changes fastest.
Arguments:
- t_query: bfloat16 [16, 2048, 4096], P('rep', 'seq'), may hold values from -45 to 45
- t_key: bfloat16 [16, 2048, 512], P('rep', 'seq'), may hold values from -4 to 4
- t_value: bfloat16 [16, 2048, 512], P('rep', 'seq'), may hold values from -6 to 6
- s_query: bfloat16 [16, 2048, 2048], P('rep', 'seq'), may hold values from -45 to 45
- s_key: bfloat16 [16, 2048, 512], P('rep', 'seq'), may hold values from -4 to 4
- student_value: bfloat16 [16, 2048, 512], P('rep', 'seq'), may hold values from -6 to 6
- student_wo: bfloat16 [2048, 2048], P('seq'), may hold values from -0.125 to 0.125
- projection: bfloat16 [4096, 2048], P('seq'), may hold values from -0.09375 to 0.09375
- doc_ids: int32 [16, 2048], P('rep'), may hold values from 0 to 15, never falling along the last dimension, each value on 1 to 512 neighbouring positions
- span_order: int32 [16, 32], P('rep'), may hold values from 0 to 31, each once within a row
Outputs:
- seq_loss: float32 [16], P('rep')
- d_wo: float32 [2048, 2048], P('seq', 'rep')
- d_query: bfloat16 [16, 2048, 2048], P('rep', 'seq')
- d_key: bfloat16 [16, 2048, 512], P('rep', 'seq')
- d_value: bfloat16 [16, 2048, 512], P('rep', 'seq')
The draws below stay inside these ranges and needn't reach their ends.
All inputs are finite; a program needn't handle non-finite values.
Results may differ from the reference program's by a relative error of at most 0.018.
The reference program's roundings to bfloat16 on the way count: a program that leaves them out, or rounds other values in their place, can miss the bound.
Values may be sent and summed in bfloat16 or wider, within the bound.
No kernel may reach another device: no remote copies, remote signals or barrier semaphores. Data moves between devices by JAX's collectives and lax.ppermute only.
A program may use at most 128 MiB of HBM per device.

```python
import math
import jax
import jax.numpy as jnp
import numpy as np
from jax import lax

HEAD_WIDTH = 128
TQH = 32
TKV = 4
STUDENT_QUERIES = 16
STUDENT_KEYS = 4
DS = 2048
DOCS = 16
SEQUENCE_LENGTH = 2048
HALVES = 32
SEQUENCE_COUNT = 16
N_SEQ = 16


def matched_couple(key, q_heads, kv_heads):
    base_key = jax.random.fold_in(key, 7)
    shape_q = (SEQUENCE_COUNT, SEQUENCE_LENGTH // 8, 8, q_heads, HEAD_WIDTH)
    shape_k = (SEQUENCE_COUNT, SEQUENCE_LENGTH // 8, 8, kv_heads, HEAD_WIDTH)
    key_vals = jnp.clip(jax.random.normal(jax.random.fold_in(base_key, 1), shape_k, jnp.float32), -4.0, 4.0)
    query_vals = jnp.clip(jax.random.normal(jax.random.fold_in(base_key, 3), shape_q, jnp.float32), -4.0, 4.0)
    return (query_vals.reshape(SEQUENCE_COUNT, SEQUENCE_LENGTH, q_heads * HEAD_WIDTH), key_vals.reshape(SEQUENCE_COUNT, SEQUENCE_LENGTH, kv_heads * HEAD_WIDTH))


def draw_t_query(key, part):
    return matched_couple(jax.random.fold_in(key, 11), TQH, TKV)[0].astype(jnp.bfloat16)


def draw_t_key(key, part):
    return matched_couple(jax.random.fold_in(key, 11), TQH, TKV)[1].astype(jnp.bfloat16)


def draw_s_query(key, part):
    return matched_couple(jax.random.fold_in(key, 12), STUDENT_QUERIES, STUDENT_KEYS)[0].astype(jnp.bfloat16)


def draw_s_key(key, part):
    return matched_couple(jax.random.fold_in(key, 12), STUDENT_QUERIES, STUDENT_KEYS)[1].astype(jnp.bfloat16)


def block_levels(key, extent, pieces, least, top_value):
    loudness, own = 1.0, jax.random.fold_in(key, 6)
    for axis_at, shards_of in pieces:
        heights = jnp.exp(jax.random.uniform(jax.random.fold_in(own, axis_at), (shards_of,), jnp.float32, least / len(pieces), top_value / len(pieces)))
        loudness = loudness * jnp.repeat(heights, extent[axis_at] // shards_of).reshape([-1 if axis == axis_at else 1 for axis in range(len(extent))])
    return loudness


def profile(count, total, most, lean):
    weights = [(1 << 20) // math.isqrt(standing ** lean) + 1 for standing in range(2, count + 1)]
    surplus, given = total - most - (count - 1), [1] * (count - 1)
    while surplus > 0:
        movable = [i for i in range(count - 1) if given[i] < most]
        whole, budget = sum([weights[i] for i in movable]), surplus
        for i in movable:
            extra = min(most - given[i], max(1, budget * weights[i] // whole), surplus)
            given[i] = given[i] + extra
            surplus = surplus - extra
    return np.array([most] + given)


def ragged(own_key, amount, total, most, skew):
    if amount == 2:
        one = jax.random.randint(own_key, (), max(1, total - most), min(most, total - 1) + 1)
        return jnp.stack([one, total - one])
    lengths = jnp.asarray(profile(amount, total, most, skew), jnp.int32)
    twos = (amount - 1) // 2
    source_of, taker = lengths[1:1 + 2 * twos:2], lengths[2:2 + 2 * twos:2]
    margin = jnp.minimum(source_of - 1, most - taker)
    moved = jax.random.randint(jax.random.fold_in(own_key, 1), (twos,), 0, 1 << 20) % (margin + 1)
    lengths = lengths.at[1:1 + 2 * twos:2].set(source_of - moved).at[2:2 + 2 * twos:2].set(taker + moved)
    return lengths[jax.random.permutation(jax.random.fold_in(own_key, 2), amount)]


def normal_values(key, shape, spread, most, cuts=(), held_as=jnp.bfloat16):
    values = spread * jax.random.normal(key, shape, jnp.float32)
    if cuts:
        values = values * block_levels(key, shape, cuts, -0.22, 0.18)
    return jnp.clip(values, -most, most).astype(held_as)


def setup_inputs(seed: int = 0) -> dict:
    arg_keys = jax.random.split(jax.random.key(seed), 11)
    t_query = draw_t_query(jax.random.fold_in(arg_keys[10], 71), 0)
    t_key = draw_t_key(jax.random.fold_in(arg_keys[10], 71), 0)
    t_value = normal_values(arg_keys[2], (SEQUENCE_COUNT, SEQUENCE_LENGTH, TKV * HEAD_WIDTH), 1.0, 6.0, ((0, 16), (1, 16)))
    s_query = draw_s_query(jax.random.fold_in(arg_keys[10], 71), 0)
    s_key = draw_s_key(jax.random.fold_in(arg_keys[10], 71), 0)
    student_value = normal_values(arg_keys[5], (SEQUENCE_COUNT, SEQUENCE_LENGTH, STUDENT_KEYS * HEAD_WIDTH), 1.0, 6.0, ((0, 16), (1, 16)))
    student_wo = normal_values(arg_keys[6], (STUDENT_QUERIES * HEAD_WIDTH, DS), (STUDENT_QUERIES * HEAD_WIDTH) ** -0.5, 0.125, ((0, 16),))
    projection = normal_values(arg_keys[7], (TQH * HEAD_WIDTH, DS), (TQH * HEAD_WIDTH) ** -0.5, 0.09375, ((0, 16),))
    doc_ids = jax.vmap(lambda own: jnp.searchsorted(jnp.cumsum(ragged(own, DOCS, SEQUENCE_LENGTH, SEQUENCE_LENGTH // 4, 2)), jnp.arange(SEQUENCE_LENGTH), side="right"))(jax.random.split(arg_keys[8], SEQUENCE_COUNT)).reshape((SEQUENCE_COUNT, SEQUENCE_LENGTH)).astype(jnp.int32)
    span_order = jax.vmap(lambda own: jax.random.permutation(own, HALVES))(jax.random.split(arg_keys[9], SEQUENCE_COUNT)).reshape((SEQUENCE_COUNT, HALVES)).astype(jnp.int32)
    return dict(t_query=t_query, t_key=t_key, t_value=t_value, s_query=s_query, s_key=s_key, student_value=student_value, student_wo=student_wo, projection=projection, doc_ids=doc_ids, span_order=span_order)


MASKED = -1e+30

def stored_positions(order_row):
    half_len = SEQUENCE_LENGTH // HALVES
    offsets = jnp.arange(half_len, dtype=jnp.int32)
    return (order_row[:, None].astype(jnp.int32) * half_len + offsets[None, :]).reshape(SEQUENCE_LENGTH)

def soft_rows(scores, allowed):
    scores = jnp.where(allowed, scores, MASKED)
    maximum = lax.optimization_barrier(jnp.max(scores, axis=1, keepdims=True))
    weights = jnp.where(allowed, jnp.exp(scores - maximum), 0.0)
    return (weights, lax.optimization_barrier(jnp.sum(weights, axis=1, keepdims=True)))

def group_sums(parts):
    per_group = parts.reshape(N_SEQ, STUDENT_QUERIES // N_SEQ, SEQUENCE_LENGTH, HEAD_WIDTH).sum(axis=1)
    rounded_result = lax.optimization_barrier(per_group.astype(jnp.bfloat16)).astype(jnp.float32)
    each_head_part = rounded_result.reshape(STUDENT_KEYS, N_SEQ // STUDENT_KEYS, SEQUENCE_LENGTH, HEAD_WIDTH).sum(axis=1).astype(jnp.bfloat16)
    return jnp.transpose(each_head_part, (1, 0, 2)).reshape(SEQUENCE_LENGTH, STUDENT_KEYS * HEAD_WIDTH)

def one_sequence(t_query, t_key, t_value, s_query, s_key, student_value, doc_row, order_row, student_wo, projection):
    scaling = 1.0 / math.sqrt(HEAD_WIDTH)
    positions = stored_positions(order_row)
    stored_docs = jnp.take(doc_row, positions)
    allowed = (stored_docs[:, None] == stored_docs[None, :]) & (positions[None, :] <= positions[:, None])
    teacher_share = TQH // TKV
    student_portion = STUDENT_QUERIES // STUDENT_KEYS

    def teacher_head(head_id):
        group_id = head_id // teacher_share
        queries = lax.dynamic_slice_in_dim(t_query, head_id * HEAD_WIDTH, HEAD_WIDTH, 1)
        key_rows = lax.dynamic_slice_in_dim(t_key, group_id * HEAD_WIDTH, HEAD_WIDTH, 1)
        val_rows = lax.dynamic_slice_in_dim(t_value, group_id * HEAD_WIDTH, HEAD_WIDTH, 1)
        scores = jnp.dot(queries, key_rows.T, preferred_element_type=jnp.float32) * scaling
        weights, totals = soft_rows(scores, allowed)
        mixed_rows = jnp.dot(weights.astype(jnp.bfloat16), val_rows, preferred_element_type=jnp.float32) / totals
        return mixed_rows.astype(jnp.bfloat16)
    teacher_ids = jnp.arange(TQH, dtype=jnp.int32)
    teacher_out = jnp.transpose(lax.map(teacher_head, teacher_ids), (1, 0, 2)).reshape(SEQUENCE_LENGTH, TQH * HEAD_WIDTH)

    def student_head(head_id):
        group_id = head_id // student_portion
        queries = lax.dynamic_slice_in_dim(s_query, head_id * HEAD_WIDTH, HEAD_WIDTH, 1)
        key_rows = lax.dynamic_slice_in_dim(s_key, group_id * HEAD_WIDTH, HEAD_WIDTH, 1)
        val_rows = lax.dynamic_slice_in_dim(student_value, group_id * HEAD_WIDTH, HEAD_WIDTH, 1)
        scores = jnp.dot(queries, key_rows.T, preferred_element_type=jnp.float32) * scaling
        weights, totals = soft_rows(scores, allowed)
        probs_h = (weights / totals).astype(jnp.bfloat16)
        mixed_rows = jnp.dot(probs_h, val_rows, preferred_element_type=jnp.float32).astype(jnp.bfloat16)
        return (probs_h, mixed_rows)
    student_ids = jnp.arange(STUDENT_QUERIES, dtype=jnp.int32)
    student_probs, student_heads = lax.map(student_head, student_ids)
    student_out = jnp.transpose(student_heads, (1, 0, 2)).reshape(SEQUENCE_LENGTH, STUDENT_QUERIES * HEAD_WIDTH)
    width_s = STUDENT_QUERIES // N_SEQ * HEAD_WIDTH
    width_t = TQH // N_SEQ * HEAD_WIDTH

    def add_group(running, group_id):
        student_part = lax.dynamic_slice_in_dim(student_out, group_id * width_s, width_s, 1)
        wo_part = lax.dynamic_slice_in_dim(student_wo, group_id * width_s, width_s, 0)
        teacher_part = lax.dynamic_slice_in_dim(teacher_out, group_id * width_t, width_t, 1)
        proj_part = lax.dynamic_slice_in_dim(projection, group_id * width_t, width_t, 0)
        term = jnp.dot(student_part, wo_part, preferred_element_type=jnp.float32) - jnp.dot(teacher_part, proj_part, preferred_element_type=jnp.float32)
        rounded_result = lax.optimization_barrier(term.astype(jnp.bfloat16))
        return (running + rounded_result.astype(jnp.float32), None)
    diff, unused = lax.scan(add_group, jnp.zeros((SEQUENCE_LENGTH, DS), jnp.float32), jnp.arange(N_SEQ, dtype=jnp.int32))
    seq_loss = jnp.sum(diff * diff) / (SEQUENCE_LENGTH * DS)
    grad_out = diff.astype(jnp.bfloat16)
    d_attn = jnp.dot(grad_out, student_wo.T, preferred_element_type=jnp.float32).astype(jnp.bfloat16)
    d_weight = jnp.dot(student_out.T, grad_out, preferred_element_type=jnp.float32)

    def student_back(items):
        head_id, probs_h, out_h = items
        group_id = head_id // student_portion
        queries = lax.dynamic_slice_in_dim(s_query, head_id * HEAD_WIDTH, HEAD_WIDTH, 1)
        key_rows = lax.dynamic_slice_in_dim(s_key, group_id * HEAD_WIDTH, HEAD_WIDTH, 1)
        val_rows = lax.dynamic_slice_in_dim(student_value, group_id * HEAD_WIDTH, HEAD_WIDTH, 1)
        grad_h = lax.dynamic_slice_in_dim(d_attn, head_id * HEAD_WIDTH, HEAD_WIDTH, 1)
        row_delta = lax.optimization_barrier(jnp.sum(grad_h.astype(jnp.float32) * out_h.astype(jnp.float32), axis=1, keepdims=True))
        d_prob = jnp.dot(grad_h, val_rows.T, preferred_element_type=jnp.float32)
        d_score = (probs_h.astype(jnp.float32) * (d_prob - row_delta)).astype(jnp.bfloat16)
        d_query = (jnp.dot(d_score, key_rows, preferred_element_type=jnp.float32) * scaling).astype(jnp.bfloat16)
        d_key = jnp.dot(d_score.T, queries, preferred_element_type=jnp.float32) * scaling
        d_value = jnp.dot(probs_h.T, grad_h, preferred_element_type=jnp.float32)
        return (d_query, d_key, d_value)
    d_query, d_key, d_value = lax.map(student_back, (student_ids, student_probs, student_heads))
    d_query = jnp.transpose(d_query, (1, 0, 2)).reshape(SEQUENCE_LENGTH, STUDENT_QUERIES * HEAD_WIDTH)
    return (seq_loss, d_weight, d_query, group_sums(d_key), group_sums(d_value))

def reference(t_query, t_key, t_value, s_query, s_key, student_value, student_wo, projection, doc_ids, span_order):

    def per_sequence(running, items):
        seq_loss, d_weight, d_query, d_key, d_value = one_sequence(*items, student_wo, projection)
        return (running + d_weight, (seq_loss, d_query, d_key, d_value))
    start_weight = jnp.zeros((STUDENT_QUERIES * HEAD_WIDTH, DS), jnp.float32)
    d_wo, stacked = lax.scan(per_sequence, start_weight, (t_query, t_key, t_value, s_query, s_key, student_value, doc_ids, span_order))
    seq_loss, d_query, d_key, d_value = stacked
    return (seq_loss, d_wo, d_query, d_key, d_value)
```

```python
import functools
import math

import jax
import jax.numpy as jnp
from jax import lax
from jax.experimental import pallas as pl
from jax.experimental.pallas import tpu as pltpu
from jax.sharding import PartitionSpec as P

D = 128
LENGTH = 2048
HALF = 64
SPANS = LENGTH // HALF
GROUPS = 16
TOKENS = LENGTH // GROUPS
WIDTH = 2048
ROWS = 256
BLOCKS = LENGTH // ROWS
STEP = 128
LIMIT = 512
SPAN = LIMIT + ROWS
STEPS = LIMIT // STEP + 1
SCALE = 1.0 / math.sqrt(D)
LOG2E = math.log2(math.e)
FAR = -1e30


def nt(a, b):
    return lax.dot_general(a, b, (((1,), (1,)), ((), ())), preferred_element_type=jnp.float32)


def nn(a, b):
    return lax.dot_general(a, b, (((1,), (0,)), ((), ())), preferred_element_type=jnp.float32)


def tn(a, b):
    return lax.dot_general(a, b, (((0,), (0,)), ((), ())), preferred_element_type=jnp.float32)


def key_steps(first_ref, block):
    return jnp.clip((block * ROWS - first_ref[block] + STEP - 1) // STEP, 0, STEPS - 1)


def each_window(first_ref, body):
    def one(block, carry):
        needed = key_steps(first_ref, block)
        for extra in range(STEPS):
            width = ROWS + extra * STEP

            @pl.when(needed == extra)
            def _():
                body(block, width)

        return carry

    lax.fori_loop(0, BLOCKS, one, 0)


def spread(order_ref, src_ref, first, dst, offset):
    cols = slice(first, first + dst.shape[1])
    if offset:
        dst[:offset, :] = jnp.zeros((offset, dst.shape[1]), dst.dtype)
    for slot in range(SPANS):
        place = pl.ds(pl.multiple_of(order_ref[slot] * HALF + offset, HALF), HALF)
        half = (slot % 2) * HALF
        dst[place, :] = src_ref[slot // 2, half : half + HALF, cols]


def window(start_ref, block, width):
    row = pl.multiple_of(block * ROWS, ROWS)
    keys = pl.ds(pl.multiple_of(row + SPAN - width, STEP), width)
    lane = lax.broadcasted_iota(jnp.int32, (ROWS, width), 1)
    line = lax.broadcasted_iota(jnp.int32, (ROWS, width), 0)
    begin = start_ref[pl.ds(row, ROWS), :] - (row + ROWS - width)
    allowed = (lane >= begin) & (lane - line <= width - ROWS)
    return pl.ds(row, ROWS), keys, jnp.where(allowed, 0.0, FAR)


def weights_of(queries, key_rows, bias):
    scores = nt(queries, key_rows) * (SCALE * LOG2E) + bias
    weights = jnp.exp2(scores - jnp.max(scores, axis=1, keepdims=True))
    return weights, jnp.sum(weights, axis=1, keepdims=True)


def put_stored(order_ref, src, out_ref, cols, offset=0, scale=None):
    for slot in range(SPANS):
        place = pl.ds(pl.multiple_of(order_ref[slot] * HALF + offset, HALF), HALF)
        value = src[place, :]
        if scale is not None:
            value = (value * scale).astype(out_ref.dtype)
        half = (slot % 2) * HALF
        out_ref[slot // 2, half : half + HALF, cols] = value


def teacher_kernel(order_ref, first_ref, start_ref, in_ref, out_ref, tq, tk, tv, to):
    spread(order_ref, in_ref, 0, tq, 0)
    spread(order_ref, in_ref, 2 * D, tk, LIMIT)
    spread(order_ref, in_ref, 3 * D, tv, LIMIT)

    def body(block, width):
        rows, keys, bias = window(start_ref, block, width)
        key_rows = tk[keys, :]
        val_rows = tv[keys, :]
        for head in range(2):
            cols = slice(head * D, (head + 1) * D)
            weights, totals = weights_of(tq[rows, cols], key_rows, bias)
            to[rows, cols] = (nn(weights.astype(jnp.bfloat16), val_rows) / totals).astype(jnp.bfloat16)

    each_window(first_ref, body)
    put_stored(order_ref, to, out_ref, slice(0, 2 * D))


def student_kernel(order_ref, first_ref, start_ref, in_ref, out_ref, probs_ref, sq, sk, sv, so):
    spread(order_ref, in_ref, 0, sq, 0)
    spread(order_ref, in_ref, D, sk, LIMIT)
    spread(order_ref, in_ref, 2 * D, sv, LIMIT)

    def body(block, width):
        rows, keys, bias = window(start_ref, block, width)
        weights, totals = weights_of(sq[rows, :], sk[keys, :], bias)
        probs = (weights * (1.0 / totals)).astype(jnp.bfloat16)
        probs_ref[block, :, SPAN - width :] = probs
        so[rows, :] = nn(probs, sv[keys, :]).astype(jnp.bfloat16)

    each_window(first_ref, body)
    put_stored(order_ref, so, out_ref, slice(0, D))


def backward_kernel(
    order_ref, first_ref, grad_ref, out_ref, in_ref, probs_ref, back_ref,
    go, so, sq, sk, sv, dq, dk, dv,
):
    spread(order_ref, grad_ref, 0, go, 0)
    spread(order_ref, out_ref, 0, so, 0)
    spread(order_ref, in_ref, 0, sq, 0)
    spread(order_ref, in_ref, D, sk, LIMIT)
    spread(order_ref, in_ref, 2 * D, sv, LIMIT)
    dk[...] = jnp.zeros_like(dk)
    dv[...] = jnp.zeros_like(dv)

    def body(block, width):
        row = pl.multiple_of(block * ROWS, ROWS)
        rows = pl.ds(row, ROWS)
        keys = pl.ds(pl.multiple_of(row + SPAN - width, STEP), width)
        probs = probs_ref[block, :, SPAN - width :]
        grads = go[rows, :]
        delta = jnp.sum(
            grads.astype(jnp.float32) * so[rows, :].astype(jnp.float32), axis=1, keepdims=True
        )
        d_probs = nt(grads, sv[keys, :])
        d_scores = (probs.astype(jnp.float32) * (d_probs - delta)).astype(jnp.bfloat16)
        dq[rows, :] = (nn(d_scores, sk[keys, :]) * SCALE).astype(jnp.bfloat16)
        dk[keys, :] += tn(d_scores, sq[rows, :])
        dv[keys, :] += tn(probs, grads)

    each_window(first_ref, body)
    put_stored(order_ref, dq, back_ref, slice(0, D))
    put_stored(order_ref, dk, back_ref, slice(D, 2 * D), LIMIT, SCALE)
    put_stored(order_ref, dv, back_ref, slice(2 * D, 3 * D), LIMIT, 1.0)


def difference_kernel(sout_ref, tout_ref, w_ref, grad_ref, attn_ref, loss_ref, attn):
    step = pl.program_id(0)
    total = None
    for group in range(GROUPS):
        wo = jnp.concatenate([w_ref[0, group, :D, :], w_ref[1, group, :D, :]], axis=1)
        pj = jnp.concatenate([w_ref[0, group, D:, :], w_ref[1, group, D:, :]], axis=1)
        term = nn(sout_ref[group], wo) - nn(tout_ref[group], pj)
        term = term.astype(jnp.bfloat16).astype(jnp.float32)
        total = term if total is None else total + term
    grad = total.astype(jnp.bfloat16)
    grad_ref[...] = grad
    loss_ref[...] = jnp.sum(total * total, axis=0, keepdims=True)
    for group in range(GROUPS):
        wo = jnp.concatenate([w_ref[0, group, :D, :], w_ref[1, group, :D, :]], axis=1)
        part = nt(grad, wo)

        @pl.when(step == 0)
        def _():
            attn[group] = part

        @pl.when(step > 0)
        def _():
            attn[group] += part

    @pl.when(step == pl.num_programs(0) - 1)
    def _():
        attn_ref[...] = attn[...].astype(jnp.bfloat16)


def weight_kernel(sout_ref, grad_ref, part_ref):
    for group in range(GROUPS):
        part = tn(sout_ref[group], grad_ref[...]).astype(jnp.bfloat16)
        part_ref[0, group] = part[:, :D]
        part_ref[1, group] = part[:, D:]


def merge_kernel(back_ref, dq_ref, dk_ref, dv_ref):
    share = GROUPS // 4
    for group in range(GROUPS):
        dq_ref[:, group * D : (group + 1) * D] = back_ref[group, :, :D]
    for head in range(4):
        cols = slice(head * D, (head + 1) * D)
        for ref, first in ((dk_ref, D), (dv_ref, 2 * D)):
            summed = back_ref[head * share, :, first : first + D].astype(jnp.float32)
            for other in range(1, share):
                summed += back_ref[head * share + other, :, first : first + D].astype(jnp.float32)
            ref[:, cols] = summed.astype(jnp.bfloat16)


def sum_kernel(parts_ref, out_ref):
    total = parts_ref[0].astype(jnp.float32)
    for group in range(1, GROUPS):
        total += parts_ref[group].astype(jnp.float32)
    out_ref[...] = total


def pack_kernel(sq_ref, sk_ref, sv_ref, tq_ref, tk_ref, tv_ref, s_ref, t_ref):
    share = GROUPS // 4
    for group in range(GROUPS):
        key = slice((group // share) * D, (group // share + 1) * D)
        s_ref[group, :, :D] = sq_ref[0, :, group * D : (group + 1) * D]
        s_ref[group, :, D : 2 * D] = sk_ref[0, :, key]
        s_ref[group, :, 2 * D :] = sv_ref[0, :, key]
        t_ref[group, :, : 2 * D] = tq_ref[0, :, 2 * group * D : 2 * (group + 1) * D]
        t_ref[group, :, 2 * D : 3 * D] = tk_ref[0, :, key]
        t_ref[group, :, 3 * D :] = tv_ref[0, :, key]


VM = pl.BlockSpec(memory_space=pltpu.VMEM)
SM = pl.BlockSpec(memory_space=pltpu.SMEM)


def bf(*shape):
    return jax.ShapeDtypeStruct(shape, jnp.bfloat16)


def fl(*shape):
    return jax.ShapeDtypeStruct(shape, jnp.float32)


def scratch(rows, cols, dtype=jnp.bfloat16):
    return pltpu.VMEM((rows, cols), dtype)


def call(kernel, outs, ins, scratches=(), scalars=0, interpret=False):
    specs = [SM] * scalars + [VM] * (len(ins) - scalars)
    single = not isinstance(outs, tuple)
    return pl.pallas_call(
        kernel,
        out_shape=outs,
        in_specs=specs,
        out_specs=VM if single else (VM,) * len(outs),
        scratch_shapes=list(scratches),
        name=kernel.__name__,
        interpret=interpret,
    )(*ins)


def difference(sout, tout, weights, interpret=False):
    return pl.pallas_call(
        difference_kernel,
        grid=(GROUPS // 2,),
        out_shape=(bf(TOKENS, WIDTH), bf(GROUPS, TOKENS, D), fl(1, WIDTH)),
        in_specs=[
            pl.BlockSpec((GROUPS, TOKENS, D), lambda r: (0, 0, 0)),
            pl.BlockSpec((GROUPS, TOKENS, 2 * D), lambda r: (0, 0, 0)),
            pl.BlockSpec((2, GROUPS, 3 * D, D), lambda r: (r, 0, 0, 0)),
        ],
        out_specs=(
            pl.BlockSpec((TOKENS, 2 * D), lambda r: (0, r)),
            pl.BlockSpec((GROUPS, TOKENS, D), lambda r: (0, 0, 0)),
            pl.BlockSpec((1, 2 * D), lambda r: (0, r)),
        ),
        scratch_shapes=[pltpu.VMEM((GROUPS, TOKENS, D), jnp.float32)],
        name="difference",
        interpret=interpret,
    )(sout, tout, weights)


def weight_parts(sout, grad, interpret=False):
    return pl.pallas_call(
        weight_kernel,
        grid=(GROUPS // 2,),
        out_shape=bf(GROUPS, GROUPS, D, D),
        in_specs=[
            pl.BlockSpec((GROUPS, TOKENS, D), lambda r: (0, 0, 0)),
            pl.BlockSpec((TOKENS, 2 * D), lambda r: (0, r)),
        ],
        out_specs=pl.BlockSpec((2, GROUPS, D, D), lambda r: (r, 0, 0, 0)),
        name="weight_parts",
        interpret=interpret,
    )(sout, grad)


def shards(
    t_query, t_key, t_value, s_query, s_key, student_value, student_wo, projection,
    doc_ids, span_order, interpret=False,
):
    run = functools.partial(call, interpret=interpret)
    rep = lax.axis_index("rep")
    order = span_order[0]
    docs = doc_ids[0]
    start = jnp.sum((docs[None, :] < docs[:, None]).astype(jnp.int32), axis=1)
    first = start[::ROWS]
    start = start[:, None]

    mine = jnp.concatenate(
        [
            lax.dynamic_slice_in_dim(student_wo, rep * D, D, 1),
            lax.dynamic_slice_in_dim(projection, rep * D, D, 1),
        ],
        axis=0,
    )
    columns = lax.all_gather(mine, "seq", axis=0)
    columns = lax.all_gather(columns.reshape(GROUPS * 3 * D, D), "rep", axis=0)
    weights = columns.reshape(-1, GROUPS, 3 * D, D)

    def swap(blocks):
        return lax.all_to_all(blocks, "seq", split_axis=0, concat_axis=0, tiled=True)

    s_pack, t_pack = run(
        pack_kernel,
        (bf(GROUPS, TOKENS, 3 * D), bf(GROUPS, TOKENS, 4 * D)),
        (s_query, s_key, student_value, t_query, t_key, t_value),
    )
    s_in = swap(s_pack)
    t_in = swap(t_pack)
    sout, probs = run(
        student_kernel,
        (bf(GROUPS, TOKENS, D), bf(BLOCKS, ROWS, SPAN)),
        (order, first, start, s_in),
        [scratch(LENGTH, D)] + [scratch(LENGTH + LIMIT, D)] * 2 + [scratch(LENGTH, D)],
        scalars=2,
    )
    s_tokens = swap(sout)
    tout = run(
        teacher_kernel,
        bf(GROUPS, TOKENS, 2 * D),
        (order, first, start, t_in),
        [scratch(LENGTH, 2 * D)] + [scratch(LENGTH + LIMIT, D)] * 2 + [scratch(LENGTH, 2 * D)],
        scalars=2,
    )
    t_tokens = swap(tout)
    grad, d_attn, squares = difference(s_tokens, t_tokens, weights, interpret=interpret)
    grads = swap(d_attn)
    seq_loss = (lax.psum(jnp.sum(squares), "seq") / (LENGTH * WIDTH)).reshape(1)
    parts = weight_parts(s_tokens, grad, interpret=interpret)
    parts = parts.reshape(-1, GROUPS * D, D)
    parts = reduce_rep(parts)
    back = run(
        backward_kernel,
        bf(GROUPS, TOKENS, 3 * D),
        (order, first, grads, sout, s_in, probs),
        [scratch(LENGTH, D)] * 3
        + [scratch(LENGTH + LIMIT, D)] * 2
        + [scratch(LENGTH, D)]
        + [scratch(LENGTH + LIMIT, D, jnp.float32)] * 2,
        scalars=2,
    )
    dq, dk, dv = run(
        merge_kernel,
        (bf(TOKENS, GROUPS * D), bf(TOKENS, 4 * D), bf(TOKENS, 4 * D)),
        (swap(back),),
    )
    d_wo = run(sum_kernel, fl(D, D), (swap(parts.reshape(GROUPS, D, D)),))
    return seq_loss, d_wo, dq[None], dk[None], dv[None]


def reduce_rep(parts):
    return lax.psum_scatter(parts, "rep", scatter_dimension=0, tiled=True)


def solution(mesh):
    tokens = P("rep", "seq", None)
    in_specs = (tokens,) * 6 + (P("seq", None),) * 2 + (P("rep", None),) * 2
    out_specs = (P("rep"), P("seq", "rep"), tokens, tokens, tokens)
    return jax.shard_map(shards, mesh=mesh, in_specs=in_specs, out_specs=out_specs, check_vma=False)
```

```python
import functools
import math

import jax
import jax.numpy as jnp
from jax import lax
from jax.experimental import pallas as pl
from jax.experimental.pallas import tpu as pltpu
from jax.sharding import PartitionSpec as P

D = 128
LENGTH = 2048
HALF = 64
SPANS = LENGTH // HALF
GROUPS = 16
RING = 8
PAIR = GROUPS // RING
TOKENS = LENGTH // GROUPS
WIDTH = 2048
BOTH = PAIR * TOKENS
COLS = 4
CHUNK = WIDTH // (2 * COLS * D)
ROWS = 256
BLOCKS = LENGTH // ROWS
STEP = 128
LIMIT = 512
SPAN = LIMIT + ROWS
STEPS = LIMIT // STEP + 1
SCALE = 1.0 / math.sqrt(D)
LOG2E = math.log2(math.e)
FAR = -1e30


def nt(a, b):
    return lax.dot_general(a, b, (((1,), (1,)), ((), ())), preferred_element_type=jnp.float32)


def nn(a, b):
    return lax.dot_general(a, b, (((1,), (0,)), ((), ())), preferred_element_type=jnp.float32)


def tn(a, b):
    return lax.dot_general(a, b, (((0,), (0,)), ((), ())), preferred_element_type=jnp.float32)


def key_steps(first_ref, block):
    return jnp.clip((block * ROWS - first_ref[block] + STEP - 1) // STEP, 0, STEPS - 1)


def each_window(first_ref, body):
    def one(block, carry):
        needed = key_steps(first_ref, block)
        for extra in range(STEPS):
            width = ROWS + extra * STEP

            @pl.when(needed == extra)
            def _():
                body(block, width)

        return carry

    lax.fori_loop(0, BLOCKS, one, 0)


def stored_slots():
    for group in range(GROUPS):
        for half in range(2):
            yield 2 * group + half, (group, half * HALF)


def ring_slots():
    for group in range(GROUPS):
        for half in range(2):
            yield 2 * group + half, (group % RING, (group // RING) * TOKENS + half * HALF)


def spread(order_ref, src_ref, first, dst, offset, slots):
    cols = slice(first, first + dst.shape[1])
    if offset:
        dst[:offset, :] = jnp.zeros((offset, dst.shape[1]), dst.dtype)
    for slot, (block, row) in slots():
        place = pl.ds(pl.multiple_of(order_ref[slot] * HALF + offset, HALF), HALF)
        dst[place, :] = src_ref[block, row : row + HALF, cols]


def window(start_ref, block, width):
    row = pl.multiple_of(block * ROWS, ROWS)
    keys = pl.ds(pl.multiple_of(row + SPAN - width, STEP), width)
    lane = lax.broadcasted_iota(jnp.int32, (ROWS, width), 1)
    line = lax.broadcasted_iota(jnp.int32, (ROWS, width), 0)
    begin = start_ref[pl.ds(row, ROWS), :] - (row + ROWS - width)
    allowed = (lane >= begin) & (lane - line <= width - ROWS)
    return pl.ds(row, ROWS), keys, jnp.where(allowed, 0.0, FAR)


def weights_of(queries, key_rows, bias):
    scores = nt(queries, key_rows) * (SCALE * LOG2E) + bias
    weights = jnp.exp2(scores - jnp.max(scores, axis=1, keepdims=True))
    return weights, jnp.sum(weights, axis=1, keepdims=True)


def put_back(order_ref, src, out_ref, cols, slots, offset=0, scale=None):
    for slot, (block, row) in slots():
        place = pl.ds(pl.multiple_of(order_ref[slot] * HALF + offset, HALF), HALF)
        value = src[place, :]
        if scale is not None:
            value = (value * scale).astype(out_ref.dtype)
        out_ref[block, row : row + HALF, cols] = value


def teacher_kernel(order_ref, first_ref, start_ref, in_ref, out_ref, tq, tk, tv, to):
    spread(order_ref, in_ref, 3 * D, tq, 0, stored_slots)
    spread(order_ref, in_ref, 5 * D, tk, LIMIT, stored_slots)
    spread(order_ref, in_ref, 6 * D, tv, LIMIT, stored_slots)

    def body(block, width):
        rows, keys, bias = window(start_ref, block, width)
        key_rows = tk[keys, :]
        val_rows = tv[keys, :]
        for head in range(2):
            cols = slice(head * D, (head + 1) * D)
            weights, totals = weights_of(tq[rows, cols], key_rows, bias)
            to[rows, cols] = (nn(weights.astype(jnp.bfloat16), val_rows) / -totals).astype(jnp.bfloat16)

    each_window(first_ref, body)
    put_back(order_ref, to, out_ref, slice(0, 2 * D), ring_slots)


def student_kernel(order_ref, first_ref, start_ref, in_ref, out_ref, probs_ref, sq, sk, sv, so):
    spread(order_ref, in_ref, 0, sq, 0, stored_slots)
    spread(order_ref, in_ref, D, sk, LIMIT, stored_slots)
    spread(order_ref, in_ref, 2 * D, sv, LIMIT, stored_slots)

    def body(block, width):
        rows, keys, bias = window(start_ref, block, width)
        weights, totals = weights_of(sq[rows, :], sk[keys, :], bias)
        probs = (weights * (1.0 / totals)).astype(jnp.bfloat16)
        probs_ref[block, :, SPAN - width :] = probs
        so[rows, :] = nn(probs, sv[keys, :]).astype(jnp.bfloat16)

    each_window(first_ref, body)
    put_back(order_ref, so, out_ref, slice(0, D), ring_slots)


def backward_kernel(
    order_ref, first_ref, grad_ref, out_ref, in_ref, probs_ref, back_ref, loss_ref,
    go, so, sq, sk, sv, dq, dk, dv,
):
    spread(order_ref, grad_ref, 0, go, 0, ring_slots)
    spread(order_ref, out_ref, 0, so, 0, ring_slots)
    spread(order_ref, in_ref, 0, sq, 0, stored_slots)
    spread(order_ref, in_ref, D, sk, LIMIT, stored_slots)
    spread(order_ref, in_ref, 2 * D, sv, LIMIT, stored_slots)
    squares = grad_ref[:, BOTH : BOTH + 8, :].astype(jnp.float32)
    loss_ref[...] = jnp.broadcast_to(jnp.sum(squares) / (LENGTH * WIDTH), (1, D))
    dk[...] = jnp.zeros_like(dk)
    dv[...] = jnp.zeros_like(dv)

    def body(block, width):
        row = pl.multiple_of(block * ROWS, ROWS)
        rows = pl.ds(row, ROWS)
        keys = pl.ds(pl.multiple_of(row + SPAN - width, STEP), width)
        probs = probs_ref[block, :, SPAN - width :]
        grads = go[rows, :]
        delta = jnp.sum(
            grads.astype(jnp.float32) * so[rows, :].astype(jnp.float32), axis=1, keepdims=True
        )
        d_probs = nt(grads, sv[keys, :])
        d_scores = (probs.astype(jnp.float32) * (d_probs - delta)).astype(jnp.bfloat16)
        dq[rows, :] = (nn(d_scores, sk[keys, :]) * SCALE).astype(jnp.bfloat16)
        dk[keys, :] += tn(d_scores, sq[rows, :])
        dv[keys, :] += tn(probs, grads)

    each_window(first_ref, body)
    put_back(order_ref, dq, back_ref, slice(0, D), stored_slots)
    put_back(order_ref, dk, back_ref, slice(D, 2 * D), stored_slots, LIMIT, SCALE)
    put_back(order_ref, dv, back_ref, slice(2 * D, 3 * D), stored_slots, LIMIT, 1.0)


def side_by_side(w_ref, group, rows):
    return jnp.concatenate([w_ref[col, group, :rows, :] for col in range(COLS)], axis=1)


def terms_kernel(sout_ref, tout_ref, w_ref, part_ref):
    total = None
    for group in range(RING):
        both = jnp.concatenate([sout_ref[group], tout_ref[group]], axis=1)
        term = nn(both, side_by_side(w_ref, group, 3 * D))
        term = term.astype(jnp.bfloat16).astype(jnp.float32)
        total = term if total is None else total + term
    part_ref[...] = total.astype(jnp.bfloat16)


def gradient_step(mine_ref, other_ref, w_ref, grad_ref):
    diff = mine_ref[...].astype(jnp.float32) + other_ref[...].astype(jnp.float32)
    grad = diff.astype(jnp.bfloat16)
    grad_ref[...] = grad
    square = jnp.sum(diff * diff, axis=0, keepdims=True)
    square = sum(square[:, col * D : (col + 1) * D] for col in range(COLS))
    wo = jnp.concatenate([side_by_side(w_ref, group, D) for group in range(RING)], axis=0)
    return nt(wo, grad), square


def first_kernel(mine_ref, other_ref, w_ref, grad_ref, attn_ref, square_ref):
    part, square = gradient_step(mine_ref, other_ref, w_ref, grad_ref)

    @pl.when(pl.program_id(0) == 0)
    def _():
        attn_ref[...] = part
        square_ref[...] = square

    @pl.when(pl.program_id(0) > 0)
    def _():
        attn_ref[...] += part
        square_ref[...] += square


def second_kernel(mine_ref, other_ref, w_ref, attn_in, square_in, grad_ref, attn_ref, attn, squares):
    part, square = gradient_step(mine_ref, other_ref, w_ref, grad_ref)
    step = pl.program_id(0)

    @pl.when(step == 0)
    def _():
        attn[...] = attn_in[...] + part
        squares[...] = square_in[...] + square

    @pl.when(step > 0)
    def _():
        attn[...] += part
        squares[...] += square

    @pl.when(step == pl.num_programs(0) - 1)
    def _():
        for group in range(RING):
            block = attn[group * D : (group + 1) * D, :]
            attn_ref[group, :BOTH, :] = block.T.astype(jnp.bfloat16)
        total = squares[...]
        high = total.astype(jnp.bfloat16).astype(jnp.float32)
        line = lax.broadcasted_iota(jnp.int32, (8, D), 0)
        rows = jnp.where(line == 0, high, jnp.where(line == 1, total - high, 0.0))
        for group in range(RING):
            attn_ref[group, BOTH:, :] = rows.astype(jnp.bfloat16)


def weight_kernel(sout_ref, first_ref, second_ref, part_ref, turned):
    step = pl.program_id(0)

    @pl.when(step == 0)
    def _():
        for group in range(RING):
            turned[group] = sout_ref[group].T

    grad = jnp.where(step < CHUNK, first_ref[...], second_ref[...])
    for group in range(RING):
        part = nn(turned[group], grad).astype(jnp.bfloat16)
        for col in range(COLS):
            part_ref[col, group] = part[:, col * D : (col + 1) * D]


def merge_kernel(back_ref, dq_ref, dk_ref, dv_ref):
    share = GROUPS // 4
    for group in range(GROUPS):
        dq_ref[:, group * D : (group + 1) * D] = back_ref[group, :, :D]
    for head in range(4):
        cols = slice(head * D, (head + 1) * D)
        for ref, first in ((dk_ref, D), (dv_ref, 2 * D)):
            summed = back_ref[head * share, :, first : first + D].astype(jnp.float32)
            for other in range(1, share):
                summed += back_ref[head * share + other, :, first : first + D].astype(jnp.float32)
            ref[:, cols] = summed.astype(jnp.bfloat16)


def sum_kernel(parts_ref, out_ref):
    total = parts_ref[0].astype(jnp.float32)
    for group in range(1, RING):
        total += parts_ref[group].astype(jnp.float32)
    out_ref[...] = total


def pack_kernel(sq_ref, sk_ref, sv_ref, tq_ref, tk_ref, tv_ref, out_ref):
    share = GROUPS // 4
    for group in range(GROUPS):
        key = slice((group // share) * D, (group // share + 1) * D)
        out_ref[group, :, :D] = sq_ref[0, :, group * D : (group + 1) * D]
        out_ref[group, :, D : 2 * D] = sk_ref[0, :, key]
        out_ref[group, :, 2 * D : 3 * D] = sv_ref[0, :, key]
        out_ref[group, :, 3 * D : 5 * D] = tq_ref[0, :, 2 * group * D : 2 * (group + 1) * D]
        out_ref[group, :, 5 * D : 6 * D] = tk_ref[0, :, key]
        out_ref[group, :, 6 * D :] = tv_ref[0, :, key]


VM = pl.BlockSpec(memory_space=pltpu.VMEM)
SM = pl.BlockSpec(memory_space=pltpu.SMEM)


def bf(*shape):
    return jax.ShapeDtypeStruct(shape, jnp.bfloat16)


def fl(*shape):
    return jax.ShapeDtypeStruct(shape, jnp.float32)


def scratch(rows, cols, dtype=jnp.bfloat16):
    return pltpu.VMEM((rows, cols), dtype)


def call(kernel, outs, ins, scratches=(), scalars=0, interpret=False):
    specs = [SM] * scalars + [VM] * (len(ins) - scalars)
    single = not isinstance(outs, tuple)
    return pl.pallas_call(
        kernel,
        out_shape=outs,
        in_specs=specs,
        out_specs=VM if single else (VM,) * len(outs),
        scratch_shapes=list(scratches),
        name=kernel.__name__,
        interpret=interpret,
    )(*ins)


def whole(*shape):
    return pl.BlockSpec(shape, lambda r: (0,) * len(shape))


def by_columns(rows):
    return pl.BlockSpec((rows, COLS * D), lambda r: (0, r))


def weight_block(rows, half):
    return pl.BlockSpec((COLS, RING, rows, D), lambda r: (r + half * CHUNK, 0, 0, 0))


def terms(sout, tout, weights, half, interpret=False):
    return pl.pallas_call(
        terms_kernel,
        grid=(CHUNK,),
        out_shape=bf(BOTH, WIDTH // 2),
        in_specs=[whole(RING, BOTH, D), whole(RING, BOTH, 2 * D), weight_block(3 * D, half)],
        out_specs=by_columns(BOTH),
        name="terms",
        interpret=interpret,
    )(sout, tout, weights)


def gradients_first(mine, other, weights, interpret=False):
    return pl.pallas_call(
        first_kernel,
        grid=(CHUNK,),
        out_shape=(bf(BOTH, WIDTH // 2), fl(RING * D, BOTH), fl(1, D)),
        in_specs=[by_columns(BOTH), by_columns(BOTH), weight_block(D, 0)],
        out_specs=(by_columns(BOTH), whole(RING * D, BOTH), whole(1, D)),
        name="gradients_first",
        interpret=interpret,
    )(mine, other, weights)


def gradients_second(mine, other, weights, attn, square, interpret=False):
    return pl.pallas_call(
        second_kernel,
        grid=(CHUNK,),
        out_shape=(bf(BOTH, WIDTH // 2), bf(RING, BOTH + 8, D)),
        in_specs=[
            by_columns(BOTH), by_columns(BOTH), weight_block(D, 1),
            whole(RING * D, BOTH), whole(1, D),
        ],
        out_specs=(by_columns(BOTH), whole(RING, BOTH + 8, D)),
        scratch_shapes=[scratch(RING * D, BOTH, jnp.float32), scratch(1, D, jnp.float32)],
        name="gradients_second",
        interpret=interpret,
    )(mine, other, weights, attn, square)


def weight_parts(sout, grad_first, grad_second, interpret=False):
    return pl.pallas_call(
        weight_kernel,
        grid=(2 * CHUNK,),
        out_shape=bf(WIDTH // D, RING, D, D),
        in_specs=[
            whole(RING, BOTH, D),
            pl.BlockSpec((BOTH, COLS * D), lambda r: (0, jnp.minimum(r, CHUNK - 1))),
            pl.BlockSpec((BOTH, COLS * D), lambda r: (0, jnp.maximum(r - CHUNK, 0))),
        ],
        out_specs=pl.BlockSpec((COLS, RING, D, D), lambda r: (r, 0, 0, 0)),
        scratch_shapes=[pltpu.VMEM((RING, D, BOTH), jnp.bfloat16)],
        name="weight_parts",
        interpret=interpret,
    )(sout, grad_first, grad_second)


def tie(value, *after):
    return lax.optimization_barrier((value,) + after)[0]


RINGS = [[ring * RING + place for place in range(RING)] for ring in range(PAIR)]
ACROSS = [(place, (place + RING) % GROUPS) for place in range(GROUPS)]


def gather_columns(student_wo, projection, swap):
    rep = lax.axis_index("rep")
    mine = jnp.concatenate(
        [
            lax.dynamic_slice_in_dim(student_wo, rep * D, D, 1),
            lax.dynamic_slice_in_dim(projection, rep * D, D, 1),
        ],
        axis=0,
    )
    pieces = swap(jnp.broadcast_to(mine, (RING,) + mine.shape))
    columns = lax.all_gather(pieces.reshape(RING * 3 * D, D), "rep", axis=0)
    return pieces, columns.reshape(-1, RING, 3 * D, D)


def shards(
    t_query, t_key, t_value, s_query, s_key, student_value, student_wo, projection,
    doc_ids, span_order, interpret=False,
):
    run = functools.partial(call, interpret=interpret)
    order = span_order[0]
    docs = doc_ids[0]
    start = jnp.sum((docs[None, :] < docs[:, None]).astype(jnp.int32), axis=1)
    first = start[::ROWS]
    start = start[:, None]

    def swap(blocks):
        return lax.all_to_all(blocks, "seq", split_axis=0, concat_axis=0, tiled=True)

    def swap_ring(blocks):
        return lax.all_to_all(
            blocks, "seq", split_axis=0, concat_axis=0, tiled=True, axis_index_groups=RINGS
        )

    pieces, weights = gather_columns(student_wo, projection, swap_ring)
    packed = run(
        pack_kernel,
        bf(GROUPS, TOKENS, 7 * D),
        (s_query, s_key, student_value, t_query, t_key, t_value),
    )
    heads_in = swap(tie(packed, pieces))
    sout, probs = run(
        student_kernel,
        (bf(RING, BOTH, D), bf(BLOCKS, ROWS, SPAN)),
        (order, first, start, heads_in),
        [scratch(LENGTH, D)] + [scratch(LENGTH + LIMIT, D)] * 2 + [scratch(LENGTH, D)],
        scalars=2,
    )
    s_tokens = swap_ring(sout)
    tout = run(
        teacher_kernel,
        bf(RING, BOTH, 2 * D),
        (order, first, start, heads_in),
        [scratch(LENGTH, 2 * D)] + [scratch(LENGTH + LIMIT, D)] * 2 + [scratch(LENGTH, 2 * D)],
        scalars=2,
    )
    t_tokens = swap_ring(tout)
    mine = [terms(s_tokens, t_tokens, weights, half, interpret=interpret) for half in range(2)]
    other = [lax.ppermute(part, "seq", ACROSS) for part in mine]
    grad_a, attn, square = gradients_first(mine[0], other[0], weights, interpret=interpret)
    grad_b, d_attn = gradients_second(
        mine[1], other[1], weights, attn, square, interpret=interpret
    )
    grads = swap_ring(d_attn)
    parts = weight_parts(s_tokens, grad_a, grad_b, interpret=interpret)
    parts = reduce_rep(parts.reshape(-1, RING * D, D))
    back, loss = run(
        backward_kernel,
        (bf(GROUPS, TOKENS, 3 * D), fl(1, D)),
        (order, first, grads, sout, heads_in, probs),
        [scratch(LENGTH, D)] * 3
        + [scratch(LENGTH + LIMIT, D)] * 2
        + [scratch(LENGTH, D)]
        + [scratch(LENGTH + LIMIT, D, jnp.float32)] * 2,
        scalars=2,
    )
    dq, dk, dv = run(
        merge_kernel,
        (bf(TOKENS, GROUPS * D), bf(TOKENS, 4 * D), bf(TOKENS, 4 * D)),
        (swap(back),),
    )
    d_wo = run(sum_kernel, fl(D, D), (swap_ring(parts.reshape(RING, D, D)),))
    return loss[0, :1], d_wo, dq[None], dk[None], dv[None]


def reduce_rep(parts):
    return lax.psum_scatter(parts, "rep", scatter_dimension=0, tiled=True)


def solution(mesh):
    tokens = P("rep", "seq", None)
    in_specs = (tokens,) * 6 + (P("seq", None),) * 2 + (P("rep", None),) * 2
    out_specs = (P("rep"), P("seq", "rep"), tokens, tokens, tokens)
    return jax.shard_map(shards, mesh=mesh, in_specs=in_specs, out_specs=out_specs, check_vma=False)
```

```python
import functools
import math

import jax
import jax.numpy as jnp
from jax import lax
from jax.experimental import pallas as pl
from jax.experimental.pallas import tpu as pltpu
from jax.sharding import PartitionSpec as P


D = 128
LENGTH = 2048
HALF = 64
GROUPS = 16
RING = 8
PAIR = GROUPS // RING
TOKENS = LENGTH // GROUPS
WIDTH = 2048
BOTH = PAIR * TOKENS
COLS = 4
PADDED = 528
CHUNK = WIDTH // (2 * COLS * D)
ROWS = 256
BLOCKS = LENGTH // ROWS
STEP = 128
LIMIT = 512
SPAN = LIMIT + ROWS
STEPS = LIMIT // STEP + 1
SCALE = 1.0 / math.sqrt(D)
LOG2E = math.log2(math.e)
FAR = -1e30


def nt(a, b):
    return lax.dot_general(a, b, (((1,), (1,)), ((), ())), preferred_element_type=jnp.float32)


def nn(a, b):
    return lax.dot_general(a, b, (((1,), (0,)), ((), ())), preferred_element_type=jnp.float32)


def tn(a, b):
    return lax.dot_general(a, b, (((0,), (0,)), ((), ())), preferred_element_type=jnp.float32)


def key_steps(first_ref, block):
    return jnp.clip((block * ROWS - first_ref[block] + STEP - 1) // STEP, 0, STEPS - 1)


def each_window(first_ref, body):
    def one(block, carry):
        needed = key_steps(first_ref, block)
        for extra in range(STEPS):
            width = ROWS + extra * STEP

            @pl.when(needed == extra)
            def _():
                body(block, width)

        return carry

    lax.fori_loop(0, BLOCKS, one, 0)


def stored_slots():
    for group in range(GROUPS):
        for half in range(2):
            yield 2 * group + half, (group, half * HALF)


def ring_slots():
    for group in range(GROUPS):
        for half in range(2):
            yield 2 * group + half, (group % RING, (group // RING) * TOKENS + half * HALF)


def spread(order_ref, src_ref, first, dst, offset, slots):
    cols = slice(first, first + dst.shape[1])
    if offset:
        dst[:offset, :] = jnp.zeros((offset, dst.shape[1]), dst.dtype)
    for slot, (block, row) in slots():
        place = pl.ds(pl.multiple_of(order_ref[slot] * HALF + offset, HALF), HALF)
        dst[place, :] = src_ref[block, row : row + HALF, cols]


def window(start_ref, block, width):
    row = pl.multiple_of(block * ROWS, ROWS)
    keys = pl.ds(pl.multiple_of(row + SPAN - width, STEP), width)
    lane = lax.broadcasted_iota(jnp.int32, (ROWS, width), 1)
    line = lax.broadcasted_iota(jnp.int32, (ROWS, width), 0)
    begin = start_ref[pl.ds(row, ROWS), :] - (row + ROWS - width)
    allowed = (lane >= begin) & (lane - line <= width - ROWS)
    return pl.ds(row, ROWS), keys, jnp.where(allowed, 0.0, FAR)


def weights_of(queries, key_rows, bias):
    scores = nt(queries, key_rows) * (SCALE * LOG2E) + bias
    weights = jnp.exp2(scores - jnp.max(scores, axis=1, keepdims=True))
    return weights, jnp.sum(weights, axis=1, keepdims=True)


def put_back(order_ref, src, out_ref, cols, slots, offset=0, scale=None):
    for slot, (block, row) in slots():
        place = pl.ds(pl.multiple_of(order_ref[slot] * HALF + offset, HALF), HALF)
        value = src[place, :]
        if scale is not None:
            value = (value * scale).astype(out_ref.dtype)
        out_ref[block, row : row + HALF, cols] = value


def teacher_kernel(order_ref, first_ref, start_ref, in_ref, out_ref, tq, tk, tv, to):
    spread(order_ref, in_ref, 3 * D, tq, 0, stored_slots)
    spread(order_ref, in_ref, 5 * D, tk, LIMIT, stored_slots)
    spread(order_ref, in_ref, 6 * D, tv, LIMIT, stored_slots)

    def body(block, width):
        rows, keys, bias = window(start_ref, block, width)
        key_rows = tk[keys, :]
        val_rows = tv[keys, :]
        for head in range(2):
            cols = slice(head * D, (head + 1) * D)
            weights, totals = weights_of(tq[rows, cols], key_rows, bias)
            to[rows, cols] = (nn(weights.astype(jnp.bfloat16), val_rows) / -totals).astype(jnp.bfloat16)

    each_window(first_ref, body)
    put_back(order_ref, to, out_ref, slice(0, 2 * D), ring_slots)


def student_kernel(order_ref, first_ref, start_ref, in_ref, out_ref, probs_ref, sq, sk, sv, so):
    spread(order_ref, in_ref, 0, sq, 0, stored_slots)
    spread(order_ref, in_ref, D, sk, LIMIT, stored_slots)
    spread(order_ref, in_ref, 2 * D, sv, LIMIT, stored_slots)

    def body(block, width):
        rows, keys, bias = window(start_ref, block, width)
        weights, totals = weights_of(sq[rows, :], sk[keys, :], bias)
        probs = (weights * (1.0 / totals)).astype(jnp.bfloat16)
        probs_ref[block, :, SPAN - width :] = probs
        so[rows, :] = nn(probs, sv[keys, :]).astype(jnp.bfloat16)

    each_window(first_ref, body)
    put_back(order_ref, so, out_ref, slice(0, D), ring_slots)


def backward_kernel(
    order_ref, first_ref, grad_ref, out_ref, in_ref, probs_ref, back_ref, loss_ref,
    go, so, sq, sk, sv, dq, dk, dv,
):
    spread(order_ref, grad_ref, 0, go, 0, ring_slots)
    spread(order_ref, out_ref, 0, so, 0, ring_slots)
    spread(order_ref, in_ref, 0, sq, 0, stored_slots)
    spread(order_ref, in_ref, D, sk, LIMIT, stored_slots)
    spread(order_ref, in_ref, 2 * D, sv, LIMIT, stored_slots)
    squares = grad_ref[:, BOTH : BOTH + 8, :].astype(jnp.float32)
    loss_ref[...] = jnp.broadcast_to(jnp.sum(squares) / (LENGTH * WIDTH), (1, D))
    dk[...] = jnp.zeros_like(dk)
    dv[...] = jnp.zeros_like(dv)

    def body(block, width):
        row = pl.multiple_of(block * ROWS, ROWS)
        rows = pl.ds(row, ROWS)
        keys = pl.ds(pl.multiple_of(row + SPAN - width, STEP), width)
        probs = probs_ref[block, :, SPAN - width :]
        grads = go[rows, :]
        delta = jnp.sum(
            grads.astype(jnp.float32) * so[rows, :].astype(jnp.float32), axis=1, keepdims=True
        )
        d_probs = nt(grads, sv[keys, :])
        d_scores = (probs.astype(jnp.float32) * (d_probs - delta)).astype(jnp.bfloat16)
        dq[rows, :] = (nn(d_scores, sk[keys, :]) * SCALE).astype(jnp.bfloat16)
        dk[keys, :] += tn(d_scores, sq[rows, :])
        dv[keys, :] += tn(probs, grads)

    each_window(first_ref, body)
    put_back(order_ref, dq, back_ref, slice(0, D), stored_slots)
    put_back(order_ref, dk, back_ref, slice(D, 2 * D), stored_slots, LIMIT, SCALE)
    put_back(order_ref, dv, back_ref, slice(2 * D, 3 * D), stored_slots, LIMIT, 1.0)


def side_by_side(w_ref, group, rows):
    return jnp.concatenate([w_ref[col, group, :rows, :] for col in range(COLS)], axis=1)


def terms_kernel(sout_ref, tout_ref, w_ref, part_ref):
    total = None
    for group in range(RING):
        both = jnp.concatenate([sout_ref[group], tout_ref[group]], axis=1)
        term = nn(both, side_by_side(w_ref, group, 3 * D))
        term = term.astype(jnp.bfloat16).astype(jnp.float32)
        total = term if total is None else total + term
    part_ref[...] = total.astype(jnp.bfloat16)


def gradient_step(mine_ref, other_ref, w_ref, grad_ref):
    diff = mine_ref[...].astype(jnp.float32) + other_ref[...].astype(jnp.float32)
    grad = diff.astype(jnp.bfloat16)
    grad_ref[...] = grad
    square = jnp.sum(diff * diff, axis=0, keepdims=True)
    square = sum(square[:, col * D : (col + 1) * D] for col in range(COLS))
    wo = jnp.concatenate([side_by_side(w_ref, group, D) for group in range(RING)], axis=0)
    return nt(wo, grad), square


def first_kernel(mine_ref, other_ref, w_ref, grad_ref, attn_ref, square_ref):
    part, square = gradient_step(mine_ref, other_ref, w_ref, grad_ref)

    @pl.when(pl.program_id(0) == 0)
    def _():
        attn_ref[...] = part
        square_ref[...] = square

    @pl.when(pl.program_id(0) > 0)
    def _():
        attn_ref[...] += part
        square_ref[...] += square


def second_kernel(mine_ref, other_ref, w_ref, attn_in, square_in, grad_ref, attn_ref, attn, squares):
    part, square = gradient_step(mine_ref, other_ref, w_ref, grad_ref)
    step = pl.program_id(0)

    @pl.when(step == 0)
    def _():
        attn[...] = attn_in[...] + part
        squares[...] = square_in[...] + square

    @pl.when(step > 0)
    def _():
        attn[...] += part
        squares[...] += square

    @pl.when(step == pl.num_programs(0) - 1)
    def _():
        for group in range(RING):
            block = attn[group * D : (group + 1) * D, :]
            attn_ref[group, :BOTH, :] = block.T.astype(jnp.bfloat16)
        total = squares[...]
        high = total.astype(jnp.bfloat16).astype(jnp.float32)
        line = lax.broadcasted_iota(jnp.int32, (8, D), 0)
        rows = jnp.where(line == 0, high, jnp.where(line == 1, total - high, 0.0))
        for group in range(RING):
            attn_ref[group, BOTH:, :] = rows.astype(jnp.bfloat16)


def weight_kernel(sout_ref, first_ref, second_ref, part_ref, turned):
    step = pl.program_id(0)

    @pl.when(step == 0)
    def _():
        for group in range(RING):
            turned[group] = sout_ref[group].T

    grad = jnp.where(step < CHUNK, first_ref[...], second_ref[...])
    for group in range(RING):
        part = nn(turned[group], grad).astype(jnp.bfloat16)
        for col in range(COLS):
            part_ref[col, group] = part[:, col * D : (col + 1) * D]


def merge_kernel(back_ref, dq_ref, dk_ref, dv_ref):
    share = GROUPS // 4
    for group in range(GROUPS):
        dq_ref[:, group * D : (group + 1) * D] = back_ref[group, :, :D]
    for head in range(4):
        cols = slice(head * D, (head + 1) * D)
        for ref, first in ((dk_ref, D), (dv_ref, 2 * D)):
            summed = back_ref[head * share, :, first : first + D].astype(jnp.float32)
            for other in range(1, share):
                summed += back_ref[head * share + other, :, first : first + D].astype(jnp.float32)
            ref[:, cols] = summed.astype(jnp.bfloat16)


def sum_kernel(parts_ref, out_ref):
    total = parts_ref[0].astype(jnp.float32)
    for group in range(1, RING):
        total += parts_ref[group].astype(jnp.float32)
    out_ref[...] = total


def pack_kernel(sq_ref, sk_ref, sv_ref, tq_ref, tk_ref, tv_ref, out_ref):
    share = GROUPS // 4
    for group in range(GROUPS):
        key = slice((group // share) * D, (group // share + 1) * D)
        out_ref[group, :, :D] = sq_ref[0, :, group * D : (group + 1) * D]
        out_ref[group, :, D : 2 * D] = sk_ref[0, :, key]
        out_ref[group, :, 2 * D : 3 * D] = sv_ref[0, :, key]
        out_ref[group, :, 3 * D : 5 * D] = tq_ref[0, :, 2 * group * D : 2 * (group + 1) * D]
        out_ref[group, :, 5 * D : 6 * D] = tk_ref[0, :, key]
        out_ref[group, :, 6 * D :] = tv_ref[0, :, key]


VM = pl.BlockSpec(memory_space=pltpu.VMEM)
SM = pl.BlockSpec(memory_space=pltpu.SMEM)


def bf(*shape):
    return jax.ShapeDtypeStruct(shape, jnp.bfloat16)


def fl(*shape):
    return jax.ShapeDtypeStruct(shape, jnp.float32)


def scratch(rows, cols, dtype=jnp.bfloat16):
    return pltpu.VMEM((rows, cols), dtype)


def call(kernel, outs, ins, scratches=(), scalars=0, interpret=False):
    specs = [SM] * scalars + [VM] * (len(ins) - scalars)
    single = not isinstance(outs, tuple)
    return pl.pallas_call(
        kernel,
        out_shape=outs,
        in_specs=specs,
        out_specs=VM if single else (VM,) * len(outs),
        scratch_shapes=list(scratches),
        interpret=interpret,
    )(*ins)


def whole(*shape):
    return pl.BlockSpec(shape, lambda r: (0,) * len(shape))


def by_columns(rows):
    return pl.BlockSpec((rows, COLS * D), lambda r: (0, r))


def weight_block(rows, half):
    return pl.BlockSpec((COLS, RING, rows, D), lambda r: (r + half * CHUNK, 0, 0, 0))


def terms(sout, tout, weights, half, interpret=False):
    return pl.pallas_call(
        terms_kernel,
        grid=(CHUNK,),
        out_shape=bf(BOTH, WIDTH // 2),
        in_specs=[whole(RING, BOTH, D), whole(RING, BOTH, 2 * D), weight_block(3 * D, half)],
        out_specs=by_columns(BOTH),
        name="terms",
        interpret=interpret,
    )(sout, tout, weights)


def gradients_first(mine, other, weights, interpret=False):
    return pl.pallas_call(
        first_kernel,
        grid=(CHUNK,),
        out_shape=(bf(BOTH, WIDTH // 2), fl(RING * D, BOTH), fl(1, D)),
        in_specs=[by_columns(BOTH), by_columns(BOTH), weight_block(D, 0)],
        out_specs=(by_columns(BOTH), whole(RING * D, BOTH), whole(1, D)),
        name="gradients_first",
        interpret=interpret,
    )(mine, other, weights)


def gradients_second(mine, other, weights, attn, square, interpret=False):
    return pl.pallas_call(
        second_kernel,
        grid=(CHUNK,),
        out_shape=(bf(BOTH, WIDTH // 2), bf(RING, BOTH + 8, D)),
        in_specs=[
            by_columns(BOTH), by_columns(BOTH), weight_block(D, 1),
            whole(RING * D, BOTH), whole(1, D),
        ],
        out_specs=(by_columns(BOTH), whole(RING, BOTH + 8, D)),
        scratch_shapes=[scratch(RING * D, BOTH, jnp.float32), scratch(1, D, jnp.float32)],
        name="gradients_second",
        interpret=interpret,
    )(mine, other, weights, attn, square)


def weight_parts(sout, grad_first, grad_second, interpret=False):
    return pl.pallas_call(
        weight_kernel,
        grid=(2 * CHUNK,),
        out_shape=bf(WIDTH // D, RING, D, D),
        in_specs=[
            whole(RING, BOTH, D),
            pl.BlockSpec((BOTH, COLS * D), lambda r: (0, jnp.minimum(r, CHUNK - 1))),
            pl.BlockSpec((BOTH, COLS * D), lambda r: (0, jnp.maximum(r - CHUNK, 0))),
        ],
        out_specs=pl.BlockSpec((COLS, RING, D, D), lambda r: (r, 0, 0, 0)),
        scratch_shapes=[pltpu.VMEM((RING, D, BOTH), jnp.bfloat16)],
        name="weight_parts",
        interpret=interpret,
    )(sout, grad_first, grad_second)


RINGS = [[ring * RING + place for place in range(RING)] for ring in range(PAIR)]
ACROSS = [(place, (place + RING) % GROUPS) for place in range(GROUPS)]


def unpad_kernel(in_ref, out_ref):
    for place in range(RING):
        out_ref[place * 3 * D : (place + 1) * 3 * D, :] = in_ref[place, : 3 * D, :]


def gather_columns(student_wo, projection, run):
    rep = lax.axis_index("rep")
    mine = jnp.concatenate(
        [
            lax.dynamic_slice_in_dim(student_wo, rep * D, D, 1),
            lax.dynamic_slice_in_dim(projection, rep * D, D, 1),
            jnp.zeros((PADDED - 3 * D, D), jnp.bfloat16),
        ],
        axis=0,
    )
    pieces = lax.all_gather(mine, "seq", axis=0, axis_index_groups=RINGS)
    pieces = run(unpad_kernel, bf(RING * 3 * D, D), (pieces,))
    columns = lax.all_gather(pieces, "rep", axis=0)
    return columns.reshape(-1, RING, 3 * D, D)


def shards(
    t_query, t_key, t_value, s_query, s_key, student_value, student_wo, projection,
    doc_ids, span_order, interpret=False,
):
    run = functools.partial(call, interpret=interpret)
    order = span_order[0]
    docs = doc_ids[0]
    start = jnp.sum((docs[None, :] < docs[:, None]).astype(jnp.int32), axis=1)
    first = start[::ROWS]
    start = start[:, None]

    def swap(blocks):
        return lax.all_to_all(blocks, "seq", split_axis=0, concat_axis=0, tiled=True)

    def swap_ring(blocks):
        return lax.all_to_all(
            blocks, "seq", split_axis=0, concat_axis=0, tiled=True, axis_index_groups=RINGS
        )

    weights = gather_columns(student_wo, projection, run)
    packed = run(
        pack_kernel,
        bf(GROUPS, TOKENS, 7 * D),
        (s_query, s_key, student_value, t_query, t_key, t_value),
    )
    heads_in = swap(packed)
    sout, probs = run(
        student_kernel,
        (bf(RING, BOTH, D), bf(BLOCKS, ROWS, SPAN)),
        (order, first, start, heads_in),
        [scratch(LENGTH, D)] + [scratch(LENGTH + LIMIT, D)] * 2 + [scratch(LENGTH, D)],
        scalars=2,
    )
    s_tokens = swap_ring(sout)
    tout = run(
        teacher_kernel,
        bf(RING, BOTH, 2 * D),
        (order, first, start, heads_in),
        [scratch(LENGTH, 2 * D)] + [scratch(LENGTH + LIMIT, D)] * 2 + [scratch(LENGTH, 2 * D)],
        scalars=2,
    )
    t_tokens = swap_ring(tout)
    mine = [terms(s_tokens, t_tokens, weights, half, interpret=interpret) for half in range(2)]
    other = [lax.ppermute(part, "seq", ACROSS) for part in mine]
    grad_a, attn, square = gradients_first(mine[0], other[0], weights, interpret=interpret)
    grad_b, d_attn = gradients_second(
        mine[1], other[1], weights, attn, square, interpret=interpret
    )
    grads = swap_ring(d_attn)
    parts = weight_parts(s_tokens, grad_a, grad_b, interpret=interpret)
    parts = reduce_rep(parts.reshape(-1, RING * D, D))
    back, loss = run(
        backward_kernel,
        (bf(GROUPS, TOKENS, 3 * D), fl(1, D)),
        (order, first, grads, sout, heads_in, probs),
        [scratch(LENGTH, D)] * 3
        + [scratch(LENGTH + LIMIT, D)] * 2
        + [scratch(LENGTH, D)]
        + [scratch(LENGTH + LIMIT, D, jnp.float32)] * 2,
        scalars=2,
    )
    dq, dk, dv = run(
        merge_kernel,
        (bf(TOKENS, GROUPS * D), bf(TOKENS, 4 * D), bf(TOKENS, 4 * D)),
        (swap(back),),
    )
    d_wo = run(sum_kernel, fl(D, D), (swap_ring(parts.reshape(RING, D, D)),))
    return loss[0, :1], d_wo, dq[None], dk[None], dv[None]


def reduce_rep(parts):
    return lax.psum_scatter(parts, "rep", scatter_dimension=0, tiled=True)


def solution(mesh):
    tokens = P("rep", "seq", None)
    in_specs = (tokens,) * 6 + (P("seq", None),) * 2 + (P("rep", None),) * 2
    out_specs = (P("rep"), P("seq", "rep"), tokens, tokens, tokens)
    return jax.shard_map(shards, mesh=mesh, in_specs=in_specs, out_specs=out_specs, check_vma=False)
```

```python
import functools
import math

import jax
import jax.numpy as jnp
from jax import lax
from jax.experimental import pallas as pl
from jax.experimental.pallas import tpu as pltpu
from jax.sharding import PartitionSpec as P


D = 128
LENGTH = 2048
HALF = 64
GROUPS = 16
RING = 8
PAIR = GROUPS // RING
TOKENS = LENGTH // GROUPS
WIDTH = 2048
BOTH = PAIR * TOKENS
COLS = 4
PADDED = 528
SIDES = WIDTH // (COLS * D)
CHUNK = WIDTH // (2 * COLS * D)
ROWS = 256
BLOCKS = LENGTH // ROWS
STEP = 128
LIMIT = 512
SPAN = LIMIT + ROWS
STEPS = LIMIT // STEP + 1
SCALE = 1.0 / math.sqrt(D)
LOG2E = math.log2(math.e)
FAR = -1e30


def nt(a, b):
    return lax.dot_general(a, b, (((1,), (1,)), ((), ())), preferred_element_type=jnp.float32)


def nn(a, b):
    return lax.dot_general(a, b, (((1,), (0,)), ((), ())), preferred_element_type=jnp.float32)


def tn(a, b):
    return lax.dot_general(a, b, (((0,), (0,)), ((), ())), preferred_element_type=jnp.float32)


def key_steps(first_ref, block):
    return jnp.clip((block * ROWS - first_ref[block] + STEP - 1) // STEP, 0, STEPS - 1)


def each_window(first_ref, body):
    def one(block, carry):
        needed = key_steps(first_ref, block)
        for extra in range(STEPS):
            width = ROWS + extra * STEP

            @pl.when(needed == extra)
            def _():
                body(block, width)

        return carry

    lax.fori_loop(0, BLOCKS, one, 0)


def stored_slots():
    for group in range(GROUPS):
        for half in range(2):
            yield 2 * group + half, (group, half * HALF)


def ring_slots():
    for group in range(GROUPS):
        for half in range(2):
            yield 2 * group + half, (group % RING, (group // RING) * TOKENS + half * HALF)


def spread(order_ref, src_ref, first, dst, offset, slots):
    cols = slice(first, first + dst.shape[1])
    if offset:
        dst[:offset, :] = jnp.zeros((offset, dst.shape[1]), dst.dtype)
    for slot, (block, row) in slots():
        place = pl.ds(pl.multiple_of(order_ref[slot] * HALF + offset, HALF), HALF)
        dst[place, :] = src_ref[block, row : row + HALF, cols]


def window(start_ref, block, width):
    row = pl.multiple_of(block * ROWS, ROWS)
    keys = pl.ds(pl.multiple_of(row + SPAN - width, STEP), width)
    lane = lax.broadcasted_iota(jnp.int32, (ROWS, width), 1)
    line = lax.broadcasted_iota(jnp.int32, (ROWS, width), 0)
    begin = start_ref[pl.ds(row, ROWS), :] - (row + ROWS - width)
    allowed = (lane >= begin) & (lane - line <= width - ROWS)
    return pl.ds(row, ROWS), keys, jnp.where(allowed, 0.0, FAR)


def weights_of(queries, key_rows, bias):
    scores = nt(queries, key_rows) * (SCALE * LOG2E) + bias
    weights = jnp.exp2(scores - jnp.max(scores, axis=1, keepdims=True))
    return weights, jnp.sum(weights, axis=1, keepdims=True)


def put_back(order_ref, src, out_ref, cols, slots, offset=0, scale=None):
    for slot, (block, row) in slots():
        place = pl.ds(pl.multiple_of(order_ref[slot] * HALF + offset, HALF), HALF)
        value = src[place, :]
        if scale is not None:
            value = (value * scale).astype(out_ref.dtype)
        out_ref[block, row : row + HALF, cols] = value


def teacher_kernel(order_ref, first_ref, start_ref, in_ref, out_ref, tq, tk, tv, to):
    spread(order_ref, in_ref, 3 * D, tq, 0, stored_slots)
    spread(order_ref, in_ref, 5 * D, tk, LIMIT, stored_slots)
    spread(order_ref, in_ref, 6 * D, tv, LIMIT, stored_slots)

    def body(block, width):
        rows, keys, bias = window(start_ref, block, width)
        key_rows = tk[keys, :]
        val_rows = tv[keys, :]
        for head in range(2):
            cols = slice(head * D, (head + 1) * D)
            weights, totals = weights_of(tq[rows, cols], key_rows, bias)
            to[rows, cols] = (nn(weights.astype(jnp.bfloat16), val_rows) / -totals).astype(jnp.bfloat16)

    each_window(first_ref, body)
    put_back(order_ref, to, out_ref, slice(0, 2 * D), ring_slots)


def student_kernel(order_ref, first_ref, start_ref, in_ref, out_ref, probs_ref, sq, sk, sv, so):
    spread(order_ref, in_ref, 0, sq, 0, stored_slots)
    spread(order_ref, in_ref, D, sk, LIMIT, stored_slots)
    spread(order_ref, in_ref, 2 * D, sv, LIMIT, stored_slots)

    def body(block, width):
        rows, keys, bias = window(start_ref, block, width)
        weights, totals = weights_of(sq[rows, :], sk[keys, :], bias)
        probs = (weights * (1.0 / totals)).astype(jnp.bfloat16)
        probs_ref[block, :, SPAN - width :] = probs
        so[rows, :] = nn(probs, sv[keys, :]).astype(jnp.bfloat16)

    each_window(first_ref, body)
    put_back(order_ref, so, out_ref, slice(0, D), ring_slots)


def backward_kernel(
    order_ref, first_ref, grad_ref, out_ref, in_ref, probs_ref, back_ref, loss_ref,
    go, so, sq, sk, sv, dq, dk, dv,
):
    spread(order_ref, grad_ref, 0, go, 0, ring_slots)
    spread(order_ref, out_ref, 0, so, 0, ring_slots)
    spread(order_ref, in_ref, 0, sq, 0, stored_slots)
    spread(order_ref, in_ref, D, sk, LIMIT, stored_slots)
    spread(order_ref, in_ref, 2 * D, sv, LIMIT, stored_slots)
    squares = grad_ref[:, BOTH : BOTH + 8, :].astype(jnp.float32)
    loss_ref[...] = jnp.broadcast_to(jnp.sum(squares) / (LENGTH * WIDTH), (1, D))
    dk[...] = jnp.zeros_like(dk)
    dv[...] = jnp.zeros_like(dv)

    def body(block, width):
        row = pl.multiple_of(block * ROWS, ROWS)
        rows = pl.ds(row, ROWS)
        keys = pl.ds(pl.multiple_of(row + SPAN - width, STEP), width)
        probs = probs_ref[block, :, SPAN - width :]
        grads = go[rows, :]
        delta = jnp.sum(
            grads.astype(jnp.float32) * so[rows, :].astype(jnp.float32), axis=1, keepdims=True
        )
        d_probs = nt(grads, sv[keys, :])
        d_scores = (probs.astype(jnp.float32) * (d_probs - delta)).astype(jnp.bfloat16)
        dq[rows, :] = (nn(d_scores, sk[keys, :]) * SCALE).astype(jnp.bfloat16)
        dk[keys, :] += tn(d_scores, sq[rows, :])
        dv[keys, :] += tn(probs, grads)

    each_window(first_ref, body)
    put_back(order_ref, dq, back_ref, slice(0, D), stored_slots)
    put_back(order_ref, dk, back_ref, slice(D, 2 * D), stored_slots, LIMIT, SCALE)
    put_back(order_ref, dv, back_ref, slice(2 * D, 3 * D), stored_slots, LIMIT, 1.0)


def side_by_side(w_ref, group, rows):
    return jnp.concatenate([w_ref[col, group, :rows, :] for col in range(COLS)], axis=1)


def terms_kernel(sout_ref, tout_ref, w_ref, part_ref):
    total = None
    for group in range(RING):
        both = jnp.concatenate([sout_ref[group], tout_ref[group]], axis=1)
        term = nn(both, side_by_side(w_ref, group, 3 * D))
        term = term.astype(jnp.bfloat16).astype(jnp.float32)
        total = term if total is None else total + term
    part_ref[...] = total.astype(jnp.bfloat16)


def gradient_step(mine_ref, other_ref, w_ref, grad_ref):
    diff = mine_ref[...].astype(jnp.float32) + other_ref[...].astype(jnp.float32)
    grad = diff.astype(jnp.bfloat16)
    grad_ref[...] = grad
    square = jnp.sum(diff * diff, axis=0, keepdims=True)
    square = sum(square[:, col * D : (col + 1) * D] for col in range(COLS))
    wo = jnp.concatenate([side_by_side(w_ref, group, D) for group in range(RING)], axis=0)
    return nt(wo, grad), square


def first_kernel(mine_ref, other_ref, w_ref, grad_ref, attn_ref, square_ref):
    part, square = gradient_step(mine_ref, other_ref, w_ref, grad_ref)

    @pl.when(pl.program_id(0) == 0)
    def _():
        attn_ref[...] = part
        square_ref[...] = square

    @pl.when(pl.program_id(0) > 0)
    def _():
        attn_ref[...] += part
        square_ref[...] += square


def second_kernel(mine_ref, other_ref, w_ref, attn_in, square_in, grad_ref, attn_ref, attn, squares):
    part, square = gradient_step(mine_ref, other_ref, w_ref, grad_ref)
    step = pl.program_id(0)

    @pl.when(step == 0)
    def _():
        attn[...] = attn_in[...] + part
        squares[...] = square_in[...] + square

    @pl.when(step > 0)
    def _():
        attn[...] += part
        squares[...] += square

    @pl.when(step == pl.num_programs(0) - 1)
    def _():
        for group in range(RING):
            block = attn[group * D : (group + 1) * D, :]
            attn_ref[group, :BOTH, :] = block.T.astype(jnp.bfloat16)
        total = squares[...]
        high = total.astype(jnp.bfloat16).astype(jnp.float32)
        line = lax.broadcasted_iota(jnp.int32, (8, D), 0)
        rows = jnp.where(line == 0, high, jnp.where(line == 1, total - high, 0.0))
        for group in range(RING):
            attn_ref[group, BOTH:, :] = rows.astype(jnp.bfloat16)


def weight_kernel(place_ref, sout_ref, first_ref, second_ref, keep_ref, send_ref, turned):
    step = pl.program_id(0)

    @pl.when(step == 0)
    def _():
        for group in range(RING):
            turned[group] = sout_ref[group].T

    grad = jnp.where(step < CHUNK, first_ref[...], second_ref[...])
    swapped = place_ref[2] == 1
    for group in range(RING):
        part = nn(turned[group], grad)
        for side in range(2):
            low = part[:, 2 * side * D : (2 * side + 1) * D]
            high = part[:, (2 * side + 1) * D : (2 * side + 2) * D]
            across = jnp.bitwise_xor(place_ref[1], side)
            keep_ref[0, across, group] = jnp.where(swapped, high, low).astype(jnp.bfloat16)
            send_ref[0, across, group] = jnp.where(swapped, low, high).astype(jnp.bfloat16)


def plus(*values):
    total = values[0].astype(jnp.float32)
    for value in values[1:]:
        total += value.astype(jnp.float32)
    return total.astype(jnp.bfloat16)


def add_core_kernel(keep_ref, other_ref, *out_refs):
    for turn, out_ref in enumerate(out_refs):
        for side in range(2):
            out_ref[side] = plus(keep_ref[turn, side], other_ref[turn, side])


def add_rows_kernel(own_ref, a_ref, b_ref, c_ref, keep_ref, send_ref):
    for side, out_ref in enumerate((keep_ref, send_ref)):
        out_ref[...] = plus(own_ref[side], a_ref[side], b_ref[side], c_ref[side])


def add_across_kernel(place_ref, own_ref, other_ref, *out_refs):
    for turn, out_ref in enumerate(out_refs):
        group = lax.rem(place_ref[3] + turn, RING)
        out_ref[...] = plus(own_ref[group], other_ref[group])


def total_kernel(*refs):
    total = refs[0][...].astype(jnp.float32)
    for ref in refs[1:-1]:
        total += ref[...].astype(jnp.float32)
    refs[-1][...] = total


def merge_kernel(back_ref, dq_ref, dk_ref, dv_ref):
    share = GROUPS // 4
    for group in range(GROUPS):
        dq_ref[:, group * D : (group + 1) * D] = back_ref[group, :, :D]
    for head in range(4):
        cols = slice(head * D, (head + 1) * D)
        for ref, first in ((dk_ref, D), (dv_ref, 2 * D)):
            summed = back_ref[head * share, :, first : first + D].astype(jnp.float32)
            for other in range(1, share):
                summed += back_ref[head * share + other, :, first : first + D].astype(jnp.float32)
            ref[:, cols] = summed.astype(jnp.bfloat16)


def pack_kernel(sq_ref, sk_ref, sv_ref, tq_ref, tk_ref, tv_ref, out_ref):
    share = GROUPS // 4
    for group in range(GROUPS):
        key = slice((group // share) * D, (group // share + 1) * D)
        out_ref[group, :, :D] = sq_ref[0, :, group * D : (group + 1) * D]
        out_ref[group, :, D : 2 * D] = sk_ref[0, :, key]
        out_ref[group, :, 2 * D : 3 * D] = sv_ref[0, :, key]
        out_ref[group, :, 3 * D : 5 * D] = tq_ref[0, :, 2 * group * D : 2 * (group + 1) * D]
        out_ref[group, :, 5 * D : 6 * D] = tk_ref[0, :, key]
        out_ref[group, :, 6 * D :] = tv_ref[0, :, key]


VM = pl.BlockSpec(memory_space=pltpu.VMEM)
SM = pl.BlockSpec(memory_space=pltpu.SMEM)


def bf(*shape):
    return jax.ShapeDtypeStruct(shape, jnp.bfloat16)


def fl(*shape):
    return jax.ShapeDtypeStruct(shape, jnp.float32)


def scratch(rows, cols, dtype=jnp.bfloat16):
    return pltpu.VMEM((rows, cols), dtype)


def call(kernel, outs, ins, scratches=(), scalars=0, interpret=False):
    specs = [SM] * scalars + [VM] * (len(ins) - scalars)
    single = not isinstance(outs, tuple)
    return pl.pallas_call(
        kernel,
        out_shape=outs,
        in_specs=specs,
        out_specs=VM if single else (VM,) * len(outs),
        scratch_shapes=list(scratches),
        interpret=interpret,
    )(*ins)


def whole(*shape):
    return pl.BlockSpec(shape, lambda r: (0,) * len(shape))


def by_columns(rows):
    return pl.BlockSpec((rows, COLS * D), lambda r: (0, r))


def weight_block(rows, half):
    return pl.BlockSpec((COLS, RING, rows, D), lambda r: (r + half * CHUNK, 0, 0, 0))


def terms(sout, tout, weights, half, interpret=False):
    return pl.pallas_call(
        terms_kernel,
        grid=(CHUNK,),
        out_shape=bf(BOTH, WIDTH // 2),
        in_specs=[whole(RING, BOTH, D), whole(RING, BOTH, 2 * D), weight_block(3 * D, half)],
        out_specs=by_columns(BOTH),
        name="terms",
        interpret=interpret,
    )(sout, tout, weights)


def gradients_first(mine, other, weights, interpret=False):
    return pl.pallas_call(
        first_kernel,
        grid=(CHUNK,),
        out_shape=(bf(BOTH, WIDTH // 2), fl(RING * D, BOTH), fl(1, D)),
        in_specs=[by_columns(BOTH), by_columns(BOTH), weight_block(D, 0)],
        out_specs=(by_columns(BOTH), whole(RING * D, BOTH), whole(1, D)),
        name="gradients_first",
        interpret=interpret,
    )(mine, other, weights)


def gradients_second(mine, other, weights, attn, square, interpret=False):
    return pl.pallas_call(
        second_kernel,
        grid=(CHUNK,),
        out_shape=(bf(BOTH, WIDTH // 2), bf(RING, BOTH + 8, D)),
        in_specs=[
            by_columns(BOTH), by_columns(BOTH), weight_block(D, 1),
            whole(RING * D, BOTH), whole(1, D),
        ],
        out_specs=(by_columns(BOTH), whole(RING, BOTH + 8, D)),
        scratch_shapes=[scratch(RING * D, BOTH, jnp.float32), scratch(1, D, jnp.float32)],
        name="gradients_second",
        interpret=interpret,
    )(mine, other, weights, attn, square)


def weight_parts(place, sout, grad_first, grad_second, interpret=False):
    turned = pl.BlockSpec(
        (1, 2, RING, D, D), lambda r, at: (lax.rem(r - at[0] + SIDES, SIDES), 0, 0, 0, 0)
    )
    return pl.pallas_call(
        weight_kernel,
        grid_spec=pltpu.PrefetchScalarGridSpec(
            num_scalar_prefetch=1,
            grid=(SIDES,),
            in_specs=[
                pl.BlockSpec((RING, BOTH, D), lambda r, at: (0, 0, 0)),
                pl.BlockSpec((BOTH, COLS * D), lambda r, at: (0, jnp.minimum(r, CHUNK - 1))),
                pl.BlockSpec((BOTH, COLS * D), lambda r, at: (0, jnp.maximum(r - CHUNK, 0))),
            ],
            out_specs=(turned, turned),
            scratch_shapes=[pltpu.VMEM((RING, D, BOTH), jnp.bfloat16)],
        ),
        out_shape=(bf(SIDES, 2, RING, D, D),) * 2,
        name="weight_parts",
        interpret=interpret,
    )(place, sout, grad_first, grad_second)


def reduce_parts(place, keep, send, run):
    reps = range(GROUPS)
    other = lax.ppermute(send, "rep", [(rep, rep ^ 1) for rep in reps])
    own, *rest = run(add_core_kernel, (bf(2, RING, D, D),) * SIDES, (keep, other))
    moved = [
        lax.ppermute(part, "rep", [(rep, (rep + turn * COLS) % GROUPS) for rep in reps])
        for turn, part in enumerate(rest, 1)
    ]
    own, send = run(add_rows_kernel, (bf(RING, D, D),) * 2, (own, *moved))
    other = lax.ppermute(send, "rep", [(rep, rep ^ 2) for rep in reps])
    own, *rest = run(add_across_kernel, (bf(D, D),) * RING, (place, own, other), scalars=1)
    moved = [
        lax.ppermute(
            part,
            "seq",
            [(at, at // RING * RING + (at + turn) % RING) for at in range(GROUPS)],
        )
        for turn, part in enumerate(rest, 1)
    ]
    return run(total_kernel, fl(D, D), (own, *moved))


RINGS = [[ring * RING + place for place in range(RING)] for ring in range(PAIR)]
ACROSS = [(place, (place + RING) % GROUPS) for place in range(GROUPS)]


def unpad_kernel(in_ref, out_ref):
    for place in range(RING):
        out_ref[place * 3 * D : (place + 1) * 3 * D, :] = in_ref[place, : 3 * D, :]


def gather_columns(student_wo, projection, run):
    rep = lax.axis_index("rep")
    mine = jnp.concatenate(
        [
            lax.dynamic_slice_in_dim(student_wo, rep * D, D, 1),
            lax.dynamic_slice_in_dim(projection, rep * D, D, 1),
            jnp.zeros((PADDED - 3 * D, D), jnp.bfloat16),
        ],
        axis=0,
    )
    pieces = lax.all_gather(mine, "seq", axis=0, axis_index_groups=RINGS)
    pieces = run(unpad_kernel, bf(RING * 3 * D, D), (pieces,))
    columns = lax.all_gather(pieces, "rep", axis=0)
    return columns.reshape(-1, RING, 3 * D, D)


def shards(
    t_query, t_key, t_value, s_query, s_key, student_value, student_wo, projection,
    doc_ids, span_order, interpret=False,
):
    run = functools.partial(call, interpret=interpret)
    order = span_order[0]
    docs = doc_ids[0]
    start = jnp.sum((docs[None, :] < docs[:, None]).astype(jnp.int32), axis=1)
    first = start[::ROWS]
    start = start[:, None]
    rep = lax.axis_index("rep")
    place = jnp.stack([rep // 4, (rep // 2) % 2, rep % 2, lax.axis_index("seq") % RING])

    def swap(blocks):
        return lax.all_to_all(blocks, "seq", split_axis=0, concat_axis=0, tiled=True)

    def swap_ring(blocks):
        return lax.all_to_all(
            blocks, "seq", split_axis=0, concat_axis=0, tiled=True, axis_index_groups=RINGS
        )

    weights = gather_columns(student_wo, projection, run)
    packed = run(
        pack_kernel,
        bf(GROUPS, TOKENS, 7 * D),
        (s_query, s_key, student_value, t_query, t_key, t_value),
    )
    heads_in = swap(packed)
    sout, probs = run(
        student_kernel,
        (bf(RING, BOTH, D), bf(BLOCKS, ROWS, SPAN)),
        (order, first, start, heads_in),
        [scratch(LENGTH, D)] + [scratch(LENGTH + LIMIT, D)] * 2 + [scratch(LENGTH, D)],
        scalars=2,
    )
    s_tokens = swap_ring(sout)
    tout = run(
        teacher_kernel,
        bf(RING, BOTH, 2 * D),
        (order, first, start, heads_in),
        [scratch(LENGTH, 2 * D)] + [scratch(LENGTH + LIMIT, D)] * 2 + [scratch(LENGTH, 2 * D)],
        scalars=2,
    )
    t_tokens = swap_ring(tout)
    mine = [terms(s_tokens, t_tokens, weights, half, interpret=interpret) for half in range(2)]
    other = [lax.ppermute(part, "seq", ACROSS) for part in mine]
    grad_a, attn, square = gradients_first(mine[0], other[0], weights, interpret=interpret)
    grad_b, d_attn = gradients_second(
        mine[1], other[1], weights, attn, square, interpret=interpret
    )
    grads = swap_ring(d_attn)
    keep, send = weight_parts(place, s_tokens, grad_a, grad_b, interpret=interpret)
    d_wo = reduce_parts(place, keep, send, run)
    back, loss = run(
        backward_kernel,
        (bf(GROUPS, TOKENS, 3 * D), fl(1, D)),
        (order, first, grads, sout, heads_in, probs),
        [scratch(LENGTH, D)] * 3
        + [scratch(LENGTH + LIMIT, D)] * 2
        + [scratch(LENGTH, D)]
        + [scratch(LENGTH + LIMIT, D, jnp.float32)] * 2,
        scalars=2,
    )
    back = swap(back)
    dq, dk, dv = run(
        merge_kernel,
        (bf(TOKENS, GROUPS * D), bf(TOKENS, 4 * D), bf(TOKENS, 4 * D)),
        (back,),
    )
    return loss[0, :1], d_wo, dq[None], dk[None], dv[None]


def solution(mesh):
    tokens = P("rep", "seq", None)
    in_specs = (tokens,) * 6 + (P("seq", None),) * 2 + (P("rep", None),) * 2
    out_specs = (P("rep"), P("seq", "rep"), tokens, tokens, tokens)
    return jax.shard_map(shards, mesh=mesh, in_specs=in_specs, out_specs=out_specs, check_vma=False)
```

```python
import functools
import math

import jax
import jax.numpy as jnp
from jax import lax
from jax.experimental import pallas as pl
from jax.experimental.pallas import tpu as pltpu
from jax.sharding import PartitionSpec as P


D = 128
LENGTH = 2048
HALF = 64
GROUPS = 16
RING = 8
PAIR = GROUPS // RING
TOKENS = LENGTH // GROUPS
WIDTH = 2048
BOTH = PAIR * TOKENS
COLS = 4
PADDED = 528
SIDES = WIDTH // (COLS * D)
CHUNK = WIDTH // (2 * COLS * D)
ROWS = 256
BLOCKS = LENGTH // ROWS
STEP = 128
LIMIT = 512
SPAN = LIMIT + ROWS
STEPS = LIMIT // STEP + 1
SCALE = 1.0 / math.sqrt(D)
LOG2E = math.log2(math.e)
FAR = -1e30


def nt(a, b):
    return lax.dot_general(a, b, (((1,), (1,)), ((), ())), preferred_element_type=jnp.float32)


def nn(a, b):
    return lax.dot_general(a, b, (((1,), (0,)), ((), ())), preferred_element_type=jnp.float32)


def tn(a, b):
    return lax.dot_general(a, b, (((0,), (0,)), ((), ())), preferred_element_type=jnp.float32)


def key_steps(first_ref, block):
    return jnp.clip((block * ROWS - first_ref[block] + STEP - 1) // STEP, 0, STEPS - 1)


def each_window(first_ref, body):
    def one(block, carry):
        needed = key_steps(first_ref, block)
        for extra in range(STEPS):
            width = ROWS + extra * STEP

            @pl.when(needed == extra)
            def _():
                body(block, width)

        return carry

    lax.fori_loop(0, BLOCKS, one, 0)


def stored_slots():
    for group in range(GROUPS):
        for half in range(2):
            yield 2 * group + half, (group, half * HALF)


def ring_slots():
    for group in range(GROUPS):
        for half in range(2):
            yield 2 * group + half, (group % RING, (group // RING) * TOKENS + half * HALF)


def spread(order_ref, src_ref, first, dst, offset, slots):
    cols = slice(first, first + dst.shape[1])
    if offset:
        dst[:offset, :] = jnp.zeros((offset, dst.shape[1]), dst.dtype)
    for slot, (block, row) in slots():
        place = pl.ds(pl.multiple_of(order_ref[slot] * HALF + offset, HALF), HALF)
        dst[place, :] = src_ref[block, row : row + HALF, cols]


def window(start_ref, block, width):
    row = pl.multiple_of(block * ROWS, ROWS)
    keys = pl.ds(pl.multiple_of(row + SPAN - width, STEP), width)
    lane = lax.broadcasted_iota(jnp.int32, (ROWS, width), 1)
    line = lax.broadcasted_iota(jnp.int32, (ROWS, width), 0)
    begin = start_ref[pl.ds(row, ROWS), :] - (row + ROWS - width)
    allowed = (lane >= begin) & (lane - line <= width - ROWS)
    return pl.ds(row, ROWS), keys, jnp.where(allowed, 0.0, FAR)


def weights_of(queries, key_rows, bias):
    scores = nt(queries, key_rows) * (SCALE * LOG2E) + bias
    weights = jnp.exp2(scores - jnp.max(scores, axis=1, keepdims=True))
    return weights, jnp.sum(weights, axis=1, keepdims=True)


def put_back(order_ref, src, out_ref, cols, slots, offset=0, scale=None):
    for slot, (block, row) in slots():
        place = pl.ds(pl.multiple_of(order_ref[slot] * HALF + offset, HALF), HALF)
        value = src[place, :]
        if scale is not None:
            value = (value * scale).astype(out_ref.dtype)
        out_ref[block, row : row + HALF, cols] = value


def teacher_kernel(order_ref, first_ref, start_ref, in_ref, out_ref, tq, tk, tv, to):
    spread(order_ref, in_ref, 0, tq, 0, stored_slots)
    spread(order_ref, in_ref, 2 * D, tk, LIMIT, stored_slots)
    spread(order_ref, in_ref, 3 * D, tv, LIMIT, stored_slots)

    def body(block, width):
        rows, keys, bias = window(start_ref, block, width)
        key_rows = tk[keys, :]
        val_rows = tv[keys, :]
        for head in range(2):
            cols = slice(head * D, (head + 1) * D)
            weights, totals = weights_of(tq[rows, cols], key_rows, bias)
            to[rows, cols] = (nn(weights.astype(jnp.bfloat16), val_rows) / -totals).astype(jnp.bfloat16)

    each_window(first_ref, body)
    put_back(order_ref, to, out_ref, slice(0, 2 * D), ring_slots)


def student_kernel(order_ref, first_ref, start_ref, in_ref, out_ref, probs_ref, sq, sk, sv, so):
    spread(order_ref, in_ref, 0, sq, 0, stored_slots)
    spread(order_ref, in_ref, D, sk, LIMIT, stored_slots)
    spread(order_ref, in_ref, 2 * D, sv, LIMIT, stored_slots)

    def body(block, width):
        rows, keys, bias = window(start_ref, block, width)
        weights, totals = weights_of(sq[rows, :], sk[keys, :], bias)
        probs = (weights * (1.0 / totals)).astype(jnp.bfloat16)
        probs_ref[block, :, SPAN - width :] = probs
        so[rows, :] = nn(probs, sv[keys, :]).astype(jnp.bfloat16)

    each_window(first_ref, body)
    put_back(order_ref, so, out_ref, slice(0, D), ring_slots)


def backward_kernel(
    order_ref, first_ref, grad_ref, out_ref, in_ref, probs_ref, back_ref, loss_ref,
    go, so, sq, sk, sv, dq, dk, dv,
):
    spread(order_ref, grad_ref, 0, go, 0, ring_slots)
    spread(order_ref, out_ref, 0, so, 0, ring_slots)
    spread(order_ref, in_ref, 0, sq, 0, stored_slots)
    spread(order_ref, in_ref, D, sk, LIMIT, stored_slots)
    spread(order_ref, in_ref, 2 * D, sv, LIMIT, stored_slots)
    squares = grad_ref[:, BOTH : BOTH + 8, :].astype(jnp.float32)
    loss_ref[...] = jnp.broadcast_to(jnp.sum(squares) / (LENGTH * WIDTH), (1, D))
    dk[...] = jnp.zeros_like(dk)
    dv[...] = jnp.zeros_like(dv)

    def body(block, width):
        row = pl.multiple_of(block * ROWS, ROWS)
        rows = pl.ds(row, ROWS)
        keys = pl.ds(pl.multiple_of(row + SPAN - width, STEP), width)
        probs = probs_ref[block, :, SPAN - width :]
        grads = go[rows, :]
        delta = jnp.sum(
            grads.astype(jnp.float32) * so[rows, :].astype(jnp.float32), axis=1, keepdims=True
        )
        d_probs = nt(grads, sv[keys, :])
        d_scores = (probs.astype(jnp.float32) * (d_probs - delta)).astype(jnp.bfloat16)
        dq[rows, :] = (nn(d_scores, sk[keys, :]) * SCALE).astype(jnp.bfloat16)
        dk[keys, :] += tn(d_scores, sq[rows, :])
        dv[keys, :] += tn(probs, grads)

    each_window(first_ref, body)
    put_back(order_ref, dq, back_ref, slice(0, D), stored_slots)
    put_back(order_ref, dk, back_ref, slice(D, 2 * D), stored_slots, LIMIT, SCALE)
    put_back(order_ref, dv, back_ref, slice(2 * D, 3 * D), stored_slots, LIMIT, 1.0)


def side_by_side(w_ref, group, rows):
    return jnp.concatenate([w_ref[col, group, :rows, :] for col in range(COLS)], axis=1)


def terms_kernel(sout_ref, tout_ref, w_ref, part_ref):
    total = None
    for group in range(RING):
        both = jnp.concatenate([sout_ref[group], tout_ref[group]], axis=1)
        term = nn(both, side_by_side(w_ref, group, 3 * D))
        term = term.astype(jnp.bfloat16).astype(jnp.float32)
        total = term if total is None else total + term
    part_ref[...] = total.astype(jnp.bfloat16)


def gradient_step(mine_ref, other_ref, w_ref, grad_ref):
    diff = mine_ref[...].astype(jnp.float32) + other_ref[...].astype(jnp.float32)
    grad = diff.astype(jnp.bfloat16)
    grad_ref[...] = grad
    square = jnp.sum(diff * diff, axis=0, keepdims=True)
    square = sum(square[:, col * D : (col + 1) * D] for col in range(COLS))
    wo = jnp.concatenate([side_by_side(w_ref, group, D) for group in range(RING)], axis=0)
    return nt(wo, grad), square


def first_kernel(mine_ref, other_ref, w_ref, grad_ref, attn_ref, square_ref):
    part, square = gradient_step(mine_ref, other_ref, w_ref, grad_ref)

    @pl.when(pl.program_id(0) == 0)
    def _():
        attn_ref[...] = part
        square_ref[...] = square

    @pl.when(pl.program_id(0) > 0)
    def _():
        attn_ref[...] += part
        square_ref[...] += square


def second_kernel(mine_ref, other_ref, w_ref, attn_in, square_in, grad_ref, attn_ref, attn, squares):
    part, square = gradient_step(mine_ref, other_ref, w_ref, grad_ref)
    step = pl.program_id(0)

    @pl.when(step == 0)
    def _():
        attn[...] = attn_in[...] + part
        squares[...] = square_in[...] + square

    @pl.when(step > 0)
    def _():
        attn[...] += part
        squares[...] += square

    @pl.when(step == pl.num_programs(0) - 1)
    def _():
        for group in range(RING):
            block = attn[group * D : (group + 1) * D, :]
            attn_ref[group, :BOTH, :] = block.T.astype(jnp.bfloat16)
        total = squares[...]
        high = total.astype(jnp.bfloat16).astype(jnp.float32)
        line = lax.broadcasted_iota(jnp.int32, (8, D), 0)
        rows = jnp.where(line == 0, high, jnp.where(line == 1, total - high, 0.0))
        for group in range(RING):
            attn_ref[group, BOTH:, :] = rows.astype(jnp.bfloat16)


def weight_kernel(place_ref, sout_ref, first_ref, second_ref, keep_ref, send_ref, turned):
    step = pl.program_id(0)

    @pl.when(step == 0)
    def _():
        for group in range(RING):
            turned[group] = sout_ref[group].T

    grad = jnp.where(step < CHUNK, first_ref[...], second_ref[...])
    swapped = place_ref[2] == 1
    for group in range(RING):
        part = nn(turned[group], grad)
        for side in range(2):
            low = part[:, 2 * side * D : (2 * side + 1) * D]
            high = part[:, (2 * side + 1) * D : (2 * side + 2) * D]
            across = jnp.bitwise_xor(place_ref[1], side)
            keep_ref[0, across, group] = jnp.where(swapped, high, low).astype(jnp.bfloat16)
            send_ref[0, across, group] = jnp.where(swapped, low, high).astype(jnp.bfloat16)


def plus(*values):
    total = values[0].astype(jnp.float32)
    for value in values[1:]:
        total += value.astype(jnp.float32)
    return total.astype(jnp.bfloat16)


def add_core_kernel(keep_ref, other_ref, *out_refs):
    def one(group, carry):
        for turn, out_ref in enumerate(out_refs):
            for side in range(2):
                out_ref[side, group] = plus(
                    keep_ref[turn, side, group], other_ref[turn, side, group]
                )
        return carry

    lax.fori_loop(0, RING, one, 0)


def add_rows_kernel(own_ref, a_ref, b_ref, c_ref, keep_ref, send_ref):
    def one(group, carry):
        for side, out_ref in enumerate((keep_ref, send_ref)):
            out_ref[group] = plus(*(ref[side, group] for ref in (own_ref, a_ref, b_ref, c_ref)))
        return carry

    lax.fori_loop(0, RING, one, 0)


def add_across_kernel(place_ref, own_ref, other_ref, *out_refs):
    for turn, out_ref in enumerate(out_refs):
        group = lax.rem(place_ref[3] + turn, RING)
        out_ref[...] = plus(own_ref[group], other_ref[group])


def total_kernel(*refs):
    total = refs[0][...].astype(jnp.float32)
    for ref in refs[1:-1]:
        total += ref[...].astype(jnp.float32)
    refs[-1][...] = total


def merge_kernel(back_ref, dq_ref, dk_ref, dv_ref):
    share = GROUPS // 4
    for group in range(GROUPS):
        dq_ref[:, group * D : (group + 1) * D] = back_ref[group, :, :D]
    for head in range(4):
        cols = slice(head * D, (head + 1) * D)
        for ref, first in ((dk_ref, D), (dv_ref, 2 * D)):
            summed = back_ref[head * share, :, first : first + D].astype(jnp.float32)
            for other in range(1, share):
                summed += back_ref[head * share + other, :, first : first + D].astype(jnp.float32)
            ref[:, cols] = summed.astype(jnp.bfloat16)


def pack_kernel(sq_ref, sk_ref, sv_ref, tq_ref, tk_ref, tv_ref, s_ref, t_ref):
    share = GROUPS // 4
    for group in range(GROUPS):
        key = slice((group // share) * D, (group // share + 1) * D)
        s_ref[group, :, :D] = sq_ref[0, :, group * D : (group + 1) * D]
        s_ref[group, :, D : 2 * D] = sk_ref[0, :, key]
        s_ref[group, :, 2 * D :] = sv_ref[0, :, key]
        t_ref[group, :, : 2 * D] = tq_ref[0, :, 2 * group * D : 2 * (group + 1) * D]
        t_ref[group, :, 2 * D : 3 * D] = tk_ref[0, :, key]
        t_ref[group, :, 3 * D :] = tv_ref[0, :, key]


VM = pl.BlockSpec(memory_space=pltpu.VMEM)
SM = pl.BlockSpec(memory_space=pltpu.SMEM)


def bf(*shape):
    return jax.ShapeDtypeStruct(shape, jnp.bfloat16)


def fl(*shape):
    return jax.ShapeDtypeStruct(shape, jnp.float32)


def scratch(rows, cols, dtype=jnp.bfloat16):
    return pltpu.VMEM((rows, cols), dtype)


def call(kernel, outs, ins, scratches=(), scalars=0, interpret=False):
    specs = [SM] * scalars + [VM] * (len(ins) - scalars)
    single = not isinstance(outs, tuple)
    return pl.pallas_call(
        kernel,
        out_shape=outs,
        in_specs=specs,
        out_specs=VM if single else (VM,) * len(outs),
        scratch_shapes=list(scratches),
        interpret=interpret,
    )(*ins)


def whole(*shape):
    return pl.BlockSpec(shape, lambda r: (0,) * len(shape))


def by_columns(rows):
    return pl.BlockSpec((rows, COLS * D), lambda r: (0, r))


def weight_block(rows, half):
    return pl.BlockSpec((COLS, RING, rows, D), lambda r: (r + half * CHUNK, 0, 0, 0))


def terms(sout, tout, weights, half, interpret=False):
    return pl.pallas_call(
        terms_kernel,
        grid=(CHUNK,),
        out_shape=bf(BOTH, WIDTH // 2),
        in_specs=[whole(RING, BOTH, D), whole(RING, BOTH, 2 * D), weight_block(3 * D, half)],
        out_specs=by_columns(BOTH),
        name="terms",
        interpret=interpret,
    )(sout, tout, weights)


def gradients_first(mine, other, weights, interpret=False):
    return pl.pallas_call(
        first_kernel,
        grid=(CHUNK,),
        out_shape=(bf(BOTH, WIDTH // 2), fl(RING * D, BOTH), fl(1, D)),
        in_specs=[by_columns(BOTH), by_columns(BOTH), weight_block(D, 0)],
        out_specs=(by_columns(BOTH), whole(RING * D, BOTH), whole(1, D)),
        name="gradients_first",
        interpret=interpret,
    )(mine, other, weights)


def gradients_second(mine, other, weights, attn, square, interpret=False):
    return pl.pallas_call(
        second_kernel,
        grid=(CHUNK,),
        out_shape=(bf(BOTH, WIDTH // 2), bf(RING, BOTH + 8, D)),
        in_specs=[
            by_columns(BOTH), by_columns(BOTH), weight_block(D, 1),
            whole(RING * D, BOTH), whole(1, D),
        ],
        out_specs=(by_columns(BOTH), whole(RING, BOTH + 8, D)),
        scratch_shapes=[scratch(RING * D, BOTH, jnp.float32), scratch(1, D, jnp.float32)],
        name="gradients_second",
        interpret=interpret,
    )(mine, other, weights, attn, square)


def weight_parts(place, sout, grad_first, grad_second, interpret=False):
    turned = pl.BlockSpec(
        (1, 2, RING, D, D), lambda r, at: (lax.rem(r - at[0] + SIDES, SIDES), 0, 0, 0, 0)
    )
    return pl.pallas_call(
        weight_kernel,
        grid_spec=pltpu.PrefetchScalarGridSpec(
            num_scalar_prefetch=1,
            grid=(SIDES,),
            in_specs=[
                pl.BlockSpec((RING, BOTH, D), lambda r, at: (0, 0, 0)),
                pl.BlockSpec((BOTH, COLS * D), lambda r, at: (0, jnp.minimum(r, CHUNK - 1))),
                pl.BlockSpec((BOTH, COLS * D), lambda r, at: (0, jnp.maximum(r - CHUNK, 0))),
            ],
            out_specs=(turned, turned),
            scratch_shapes=[pltpu.VMEM((RING, D, BOTH), jnp.bfloat16)],
        ),
        out_shape=(bf(SIDES, 2, RING, D, D),) * 2,
        name="weight_parts",
        interpret=interpret,
    )(place, sout, grad_first, grad_second)


def reduce_parts(place, keep, send, run):
    reps = range(GROUPS)
    other = lax.ppermute(send, "rep", [(rep, rep ^ 1) for rep in reps])
    own, *rest = run(add_core_kernel, (bf(2, RING, D, D),) * SIDES, (keep, other))
    moved = []
    for turn, part in enumerate(rest, 1):
        moved.append(
            lax.ppermute(part, "rep", [(rep, (rep + turn * COLS) % GROUPS) for rep in reps])
        )
    own, send = run(add_rows_kernel, (bf(RING, D, D),) * 2, (own, *moved))
    other = lax.ppermute(send, "rep", [(rep, rep ^ 2) for rep in reps])
    own, *rest = run(add_across_kernel, (bf(D, D),) * RING, (place, own, other), scalars=1)
    moved = [
        lax.ppermute(
            part,
            "seq",
            [(at, at // RING * RING + (at + turn) % RING) for at in range(GROUPS)],
        )
        for turn, part in enumerate(rest, 1)
    ]
    return run(total_kernel, fl(D, D), (own, *moved))


def tie(value, *after):
    return lax.optimization_barrier((value,) + after)[0]


RINGS = [[ring * RING + place for place in range(RING)] for ring in range(PAIR)]
ACROSS = [(place, (place + RING) % GROUPS) for place in range(GROUPS)]


def unpad_kernel(in_ref, out_ref):
    for place in range(RING):
        out_ref[place * 3 * D : (place + 1) * 3 * D, :] = in_ref[place, : 3 * D, :]


def gather_columns(student_wo, projection, run):
    rep = lax.axis_index("rep")
    mine = jnp.concatenate(
        [
            lax.dynamic_slice_in_dim(student_wo, rep * D, D, 1),
            lax.dynamic_slice_in_dim(projection, rep * D, D, 1),
            jnp.zeros((PADDED - 3 * D, D), jnp.bfloat16),
        ],
        axis=0,
    )
    pieces = lax.all_gather(mine, "seq", axis=0, axis_index_groups=RINGS)
    pieces = run(unpad_kernel, bf(RING * 3 * D, D), (pieces,))
    columns = lax.all_gather(pieces, "rep", axis=0)
    return columns.reshape(-1, RING, 3 * D, D)


def shards(
    t_query, t_key, t_value, s_query, s_key, student_value, student_wo, projection,
    doc_ids, span_order, interpret=False,
):
    run = functools.partial(call, interpret=interpret)
    order = span_order[0]
    docs = doc_ids[0]
    start = jnp.sum((docs[None, :] < docs[:, None]).astype(jnp.int32), axis=1)
    first = start[::ROWS]
    start = start[:, None]
    rep = lax.axis_index("rep")
    place = jnp.stack([rep // 4, (rep // 2) % 2, rep % 2, lax.axis_index("seq") % RING])

    def swap(blocks):
        return lax.all_to_all(blocks, "seq", split_axis=0, concat_axis=0, tiled=True)

    def swap_ring(blocks):
        return lax.all_to_all(
            blocks, "seq", split_axis=0, concat_axis=0, tiled=True, axis_index_groups=RINGS
        )

    weights = gather_columns(student_wo, projection, run)
    s_pack, t_pack = run(
        pack_kernel,
        (bf(GROUPS, TOKENS, 3 * D), bf(GROUPS, TOKENS, 4 * D)),
        (s_query, s_key, student_value, t_query, t_key, t_value),
    )
    s_in = swap(s_pack)
    t_in = swap(tie(t_pack, s_in))
    sout, probs = run(
        student_kernel,
        (bf(RING, BOTH, D), bf(BLOCKS, ROWS, SPAN)),
        (order, first, start, s_in),
        [scratch(LENGTH, D)] + [scratch(LENGTH + LIMIT, D)] * 2 + [scratch(LENGTH, D)],
        scalars=2,
    )
    s_tokens = swap_ring(tie(sout, t_in))
    tout = run(
        teacher_kernel,
        bf(RING, BOTH, 2 * D),
        (order, first, start, t_in),
        [scratch(LENGTH, 2 * D)] + [scratch(LENGTH + LIMIT, D)] * 2 + [scratch(LENGTH, 2 * D)],
        scalars=2,
    )
    t_tokens = swap_ring(tout)
    mine = [terms(s_tokens, t_tokens, weights, half, interpret=interpret) for half in range(2)]
    other = [lax.ppermute(part, "seq", ACROSS) for part in mine]
    grad_a, attn, square = gradients_first(mine[0], other[0], weights, interpret=interpret)
    grad_b, d_attn = gradients_second(
        mine[1], other[1], weights, attn, square, interpret=interpret
    )
    grads = swap_ring(d_attn)
    keep, send = weight_parts(place, s_tokens, grad_a, grad_b, interpret=interpret)
    d_wo = reduce_parts(place, keep, send, run)
    back, loss = run(
        backward_kernel,
        (bf(GROUPS, TOKENS, 3 * D), fl(1, D)),
        (order, first, grads, sout, s_in, probs),
        [scratch(LENGTH, D)] * 3
        + [scratch(LENGTH + LIMIT, D)] * 2
        + [scratch(LENGTH, D)]
        + [scratch(LENGTH + LIMIT, D, jnp.float32)] * 2,
        scalars=2,
    )
    back = swap(back)
    dq, dk, dv = run(
        merge_kernel,
        (bf(TOKENS, GROUPS * D), bf(TOKENS, 4 * D), bf(TOKENS, 4 * D)),
        (back,),
    )
    return loss[0, :1], d_wo, dq[None], dk[None], dv[None]


def solution(mesh):
    tokens = P("rep", "seq", None)
    in_specs = (tokens,) * 6 + (P("seq", None),) * 2 + (P("rep", None),) * 2
    out_specs = (P("rep"), P("seq", "rep"), tokens, tokens, tokens)
    return jax.shard_map(shards, mesh=mesh, in_specs=in_specs, out_specs=out_specs, check_vma=False)
```

```python
import functools
import math

import jax
import jax.numpy as jnp
from jax import lax
from jax.experimental import pallas as pl
from jax.experimental.pallas import tpu as pltpu
from jax.sharding import PartitionSpec as P


D = 128
LENGTH = 2048
HALF = 64
GROUPS = 16
RING = 8
PAIR = GROUPS // RING
TOKENS = LENGTH // GROUPS
WIDTH = 2048
BOTH = PAIR * TOKENS
COLS = 4
SIDES = WIDTH // (COLS * D)
CHUNK = WIDTH // (2 * COLS * D)
HALF_COLS = COLS * CHUNK
ROWS = 256
BLOCKS = LENGTH // ROWS
STEP = 128
LIMIT = 512
SPAN = LIMIT + ROWS
SCALE = 1.0 / math.sqrt(D)
LOG2E = math.log2(math.e)
FAR = -1e30


def nt(a, b):
    return lax.dot_general(a, b, (((1,), (1,)), ((), ())), preferred_element_type=jnp.float32)


def nn(a, b):
    return lax.dot_general(a, b, (((1,), (0,)), ((), ())), preferred_element_type=jnp.float32)


def tn(a, b):
    return lax.dot_general(a, b, (((0,), (0,)), ((), ())), preferred_element_type=jnp.float32)


def each_window(first_ref, body, step):
    def one(block, carry):
        needed = (block * ROWS - first_ref[block] + step - 1) // step
        needed = jnp.clip(needed, 0, LIMIT // step)
        for extra in range(LIMIT // step + 1):

            @pl.when(needed == extra)
            def _():
                body(block, ROWS + extra * step)

        return carry

    lax.fori_loop(0, BLOCKS, one, 0)


def stored_slots():
    for group in range(GROUPS):
        for half in range(2):
            yield 2 * group + half, (group, half * HALF)


def ring_slots():
    for group in range(GROUPS):
        for half in range(2):
            yield 2 * group + half, (group % RING, (group // RING) * TOKENS + half * HALF)


def spread(order_ref, src_ref, first, dst, offset, slots):
    cols = slice(first, first + dst.shape[1])
    if offset:
        dst[:offset, :] = jnp.zeros((offset, dst.shape[1]), dst.dtype)
    for slot, (block, row) in slots():
        place = pl.ds(pl.multiple_of(order_ref[slot] * HALF + offset, HALF), HALF)
        dst[place, :] = src_ref[block, row : row + HALF, cols]


def window(start_ref, block, width):
    row = pl.multiple_of(block * ROWS, ROWS)
    keys = pl.ds(pl.multiple_of(row + SPAN - width, STEP), width)
    lane = lax.broadcasted_iota(jnp.int32, (ROWS, width), 1)
    line = lax.broadcasted_iota(jnp.int32, (ROWS, width), 0)
    begin = start_ref[pl.ds(row, ROWS), :] - (row + ROWS - width)
    allowed = (lane >= begin) & (lane - line <= width - ROWS)
    return pl.ds(row, ROWS), keys, jnp.where(allowed, 0.0, FAR)


def weights_of(queries, key_rows, bias):
    scores = nt(queries, key_rows) * (SCALE * LOG2E) + bias
    weights = jnp.exp2(scores - jnp.max(scores, axis=1, keepdims=True))
    return weights, jnp.sum(weights, axis=1, keepdims=True)


def put_back(order_ref, src, out_ref, cols, slots, offset=0, scale=None):
    for slot, (block, row) in slots():
        place = pl.ds(pl.multiple_of(order_ref[slot] * HALF + offset, HALF), HALF)
        value = src[place, :]
        if scale is not None:
            value = (value * scale).astype(out_ref.dtype)
        out_ref[block, row : row + HALF, cols] = value


def teacher_kernel(order_ref, first_ref, start_ref, in_ref, out_ref, tq, tk, tv, to):
    spread(order_ref, in_ref, 0, tq, 0, stored_slots)
    spread(order_ref, in_ref, 2 * D, tk, LIMIT, stored_slots)
    spread(order_ref, in_ref, 3 * D, tv, LIMIT, stored_slots)

    def body(block, width):
        rows, keys, bias = window(start_ref, block, width)
        key_rows = tk[keys, :]
        val_rows = tv[keys, :]
        for head in range(2):
            cols = slice(head * D, (head + 1) * D)
            weights, totals = weights_of(tq[rows, cols], key_rows, bias)
            to[rows, cols] = (nn(weights.astype(jnp.bfloat16), val_rows) / -totals).astype(jnp.bfloat16)

    each_window(first_ref, body, 2 * STEP)
    put_back(order_ref, to, out_ref, slice(0, 2 * D), ring_slots)


def student_kernel(order_ref, first_ref, start_ref, in_ref, out_ref, probs_ref, sq, sk, sv, so):
    spread(order_ref, in_ref, 0, sq, 0, stored_slots)
    spread(order_ref, in_ref, D, sk, LIMIT, stored_slots)
    spread(order_ref, in_ref, 2 * D, sv, LIMIT, stored_slots)

    def body(block, width):
        rows, keys, bias = window(start_ref, block, width)
        weights, totals = weights_of(sq[rows, :], sk[keys, :], bias)
        probs = (weights * (1.0 / totals)).astype(jnp.bfloat16)
        probs_ref[block, :, SPAN - width :] = probs
        so[rows, :] = nn(probs, sv[keys, :]).astype(jnp.bfloat16)

    each_window(first_ref, body, 2 * STEP)
    put_back(order_ref, so, out_ref, slice(0, D), ring_slots)


def backward_kernel(
    order_ref, first_ref, grad_ref, out_ref, in_ref, probs_ref, back_ref, loss_ref,
    go, so, sq, sk, sv, dq, dk, dv,
):
    spread(order_ref, grad_ref, 0, go, 0, ring_slots)
    spread(order_ref, out_ref, 0, so, 0, ring_slots)
    spread(order_ref, in_ref, 0, sq, 0, stored_slots)
    spread(order_ref, in_ref, D, sk, LIMIT, stored_slots)
    spread(order_ref, in_ref, 2 * D, sv, LIMIT, stored_slots)
    squares = grad_ref[:, BOTH : BOTH + 8, :].astype(jnp.float32)
    loss_ref[...] = jnp.broadcast_to(jnp.sum(squares) / (LENGTH * WIDTH), (1, D))
    dk[...] = jnp.zeros_like(dk)
    dv[...] = jnp.zeros_like(dv)

    def body(block, width):
        row = pl.multiple_of(block * ROWS, ROWS)
        rows = pl.ds(row, ROWS)
        keys = pl.ds(pl.multiple_of(row + SPAN - width, STEP), width)
        probs = probs_ref[block, :, SPAN - width :]
        grads = go[rows, :]
        delta = jnp.sum(
            grads.astype(jnp.float32) * so[rows, :].astype(jnp.float32), axis=1, keepdims=True
        )
        d_probs = nt(grads, sv[keys, :])
        d_scores = (probs.astype(jnp.float32) * (d_probs - delta)).astype(jnp.bfloat16)
        dq[rows, :] = (nn(d_scores, sk[keys, :]) * SCALE).astype(jnp.bfloat16)
        dk[keys, :] += tn(d_scores, sq[rows, :])
        dv[keys, :] += tn(probs, grads)

    each_window(first_ref, body, STEP)
    put_back(order_ref, dq, back_ref, slice(0, D), stored_slots)
    put_back(order_ref, dk, back_ref, slice(D, 2 * D), stored_slots, LIMIT, SCALE)
    put_back(order_ref, dv, back_ref, slice(2 * D, 3 * D), stored_slots, LIMIT, 1.0)


def side_by_side(refs, rows):
    return jnp.concatenate([ref[side, 0, :rows, :] for ref in refs for side in range(2)], axis=1)


def terms_kernel(sout_ref, tout_ref, a_ref, b_ref, c_ref, d_ref, part_ref, total):
    both = jnp.concatenate([sout_ref[0], tout_ref[0]], axis=1)
    term = nn(both, side_by_side((a_ref, b_ref, c_ref, d_ref), 3 * D))
    term = term.astype(jnp.bfloat16).astype(jnp.float32)

    @pl.when(pl.program_id(0) == 0)
    def _():
        total[...] = term

    @pl.when(pl.program_id(0) > 0)
    def _():
        total[...] += term

    @pl.when(pl.program_id(0) == RING - 1)
    def _():
        part_ref[...] = total[...].astype(jnp.bfloat16)


def gradient_once(mine_ref, other_ref, grad_ref, square_ref):
    diff = mine_ref[...].astype(jnp.float32) + other_ref[...].astype(jnp.float32)
    grad_ref[...] = diff.astype(jnp.bfloat16)
    square = jnp.sum(diff * diff, axis=0, keepdims=True)
    square_ref[...] = sum(square[:, col * D : (col + 1) * D] for col in range(HALF_COLS))


def first_kernel(
    mine_ref, other_ref, a_ref, b_ref, c_ref, d_ref, grad_ref, attn_ref, square_ref
):
    @pl.when(pl.program_id(0) == 0)
    def _():
        gradient_once(mine_ref, other_ref, grad_ref, square_ref)

    attn_ref[0] = nt(side_by_side((a_ref, b_ref, c_ref, d_ref), D), grad_ref[...])


def second_kernel(
    mine_ref, other_ref, a_ref, b_ref, c_ref, d_ref, attn_in, square_in, grad_ref, attn_ref,
    squares,
):
    @pl.when(pl.program_id(0) == 0)
    def _():
        gradient_once(mine_ref, other_ref, grad_ref, squares)
        squares[...] += square_in[...]

    part = nt(side_by_side((a_ref, b_ref, c_ref, d_ref), D), grad_ref[...]) + attn_in[0]
    attn_ref[0, :BOTH, :] = part.T.astype(jnp.bfloat16)
    total = squares[...]
    high = total.astype(jnp.bfloat16).astype(jnp.float32)
    line = lax.broadcasted_iota(jnp.int32, (8, D), 0)
    rows = jnp.where(line == 0, high, jnp.where(line == 1, total - high, 0.0))
    attn_ref[0, BOTH:, :] = rows.astype(jnp.bfloat16)


def weight_kernel(sout_ref, first_ref, second_ref, keep_ref, send_ref, turned):
    step = pl.program_id(0)

    @pl.when(step == 0)
    def _():
        for group in range(RING):
            turned[group] = sout_ref[group].T

    grad = jnp.where(step < CHUNK, first_ref[...], second_ref[...])

    def one(pair, carry):
        for half in range(2):
            group = 2 * pair + half
            part = nn(turned[group], grad).astype(jnp.bfloat16)
            for side in range(2):
                keep_ref[0, side, group] = part[:, side * D : (side + 1) * D]
                send_ref[0, side, group] = part[:, (2 + side) * D : (3 + side) * D]
        return carry

    lax.fori_loop(0, RING // 2, one, 0)


def gather_kernel(place_ref, own_ref, *refs):
    out_ref = refs[-1]
    out_ref[place_ref[0]] = own_ref[...]
    for turn, ref in enumerate(refs[:-1], 1):
        out_ref[lax.rem(place_ref[0] - turn + RING, RING)] = ref[...]


def join_kernel(own_ref, other_ref, out_ref):
    def one(group, carry):
        out_ref[0, group] = own_ref[group]
        out_ref[1, group] = other_ref[group]
        return carry

    lax.fori_loop(0, RING, one, 0)


def plus(*values):
    total = values[0].astype(jnp.float32)
    for value in values[1:]:
        total += value.astype(jnp.float32)
    return total.astype(jnp.bfloat16)


def add_core_kernel(keep_ref, other_ref, *out_refs):
    def one(group, carry):
        for turn, out_ref in enumerate(out_refs):
            for side in range(2):
                out_ref[side, group] = plus(
                    keep_ref[turn, side, group], other_ref[turn, side, group]
                )
        return carry

    lax.fori_loop(0, RING, one, 0)


def add_rows_kernel(own_ref, a_ref, b_ref, c_ref, keep_ref, send_ref):
    def one(group, carry):
        for side, out_ref in enumerate((keep_ref, send_ref)):
            out_ref[group] = plus(*(ref[side, group] for ref in (own_ref, a_ref, b_ref, c_ref)))
        return carry

    lax.fori_loop(0, RING, one, 0)


def add_across_kernel(place_ref, own_ref, other_ref, *out_refs):
    for turn, out_ref in enumerate(out_refs):
        group = lax.rem(place_ref[0] + turn, RING)
        out_ref[...] = plus(own_ref[group], other_ref[group])


def total_kernel(*refs):
    total = refs[0][...].astype(jnp.float32)
    for ref in refs[1:-1]:
        total += ref[...].astype(jnp.float32)
    refs[-1][...] = total


def merge_kernel(back_ref, dq_ref, dk_ref, dv_ref):
    share = GROUPS // 4
    for group in range(GROUPS):
        dq_ref[:, group * D : (group + 1) * D] = back_ref[group, :, :D]
    for head in range(4):
        cols = slice(head * D, (head + 1) * D)
        for ref, first in ((dk_ref, D), (dv_ref, 2 * D)):
            summed = back_ref[head * share, :, first : first + D].astype(jnp.float32)
            for other in range(1, share):
                summed += back_ref[head * share + other, :, first : first + D].astype(jnp.float32)
            ref[:, cols] = summed.astype(jnp.bfloat16)


def pack_kernel(sq_ref, sk_ref, sv_ref, tq_ref, tk_ref, tv_ref, s_ref, t_ref):
    share = GROUPS // 4

    def one(head, carry):
        key = pl.ds(pl.multiple_of(head * D, D), D)
        for member in range(share):
            group = head * share + member
            start = pl.multiple_of(group * D, D)
            s_ref[group, :, :D] = sq_ref[0, :, pl.ds(start, D)]
            s_ref[group, :, D : 2 * D] = sk_ref[0, :, key]
            s_ref[group, :, 2 * D :] = sv_ref[0, :, key]
            start = pl.multiple_of(2 * group * D, 2 * D)
            t_ref[group, :, : 2 * D] = tq_ref[0, :, pl.ds(start, 2 * D)]
            t_ref[group, :, 2 * D : 3 * D] = tk_ref[0, :, key]
            t_ref[group, :, 3 * D :] = tv_ref[0, :, key]
        return carry

    lax.fori_loop(0, 4, one, 0)


VM = pl.BlockSpec(memory_space=pltpu.VMEM)
SM = pl.BlockSpec(memory_space=pltpu.SMEM)


def bf(*shape):
    return jax.ShapeDtypeStruct(shape, jnp.bfloat16)


def fl(*shape):
    return jax.ShapeDtypeStruct(shape, jnp.float32)


def scratch(rows, cols, dtype=jnp.bfloat16):
    return pltpu.VMEM((rows, cols), dtype)


def call(kernel, outs, ins, scratches=(), scalars=0, interpret=False):
    specs = [SM] * scalars + [VM] * (len(ins) - scalars)
    single = not isinstance(outs, tuple)
    return pl.pallas_call(
        kernel,
        out_shape=outs,
        in_specs=specs,
        out_specs=VM if single else (VM,) * len(outs),
        scratch_shapes=list(scratches),
        interpret=interpret,
    )(*ins)


def whole(*shape):
    return pl.BlockSpec(shape, lambda r: (0,) * len(shape))


def by_group(*shape):
    return pl.BlockSpec((1,) + shape, lambda g: (g,) + (0,) * len(shape))


def weight_blocks(rows):
    return [pl.BlockSpec((2, 1, rows, D), lambda g: (0, g, 0, 0))] * 4


def terms(sout, tout, weights, interpret=False):
    return pl.pallas_call(
        terms_kernel,
        grid=(RING,),
        out_shape=bf(BOTH, WIDTH // 2),
        in_specs=[by_group(BOTH, D), by_group(BOTH, 2 * D)] + weight_blocks(3 * D),
        out_specs=whole(BOTH, WIDTH // 2),
        scratch_shapes=[scratch(BOTH, WIDTH // 2, jnp.float32)],
        name="terms",
        interpret=interpret,
    )(sout, tout, *weights)


def gradients_first(mine, other, weights, interpret=False):
    half = whole(BOTH, WIDTH // 2)
    return pl.pallas_call(
        first_kernel,
        grid=(RING,),
        out_shape=(bf(BOTH, WIDTH // 2), fl(RING, D, BOTH), fl(1, D)),
        in_specs=[half, half] + weight_blocks(D),
        out_specs=(half, by_group(D, BOTH), whole(1, D)),
        name="gradients_first",
        interpret=interpret,
    )(mine, other, *weights)


def gradients_second(mine, other, weights, attn, square, interpret=False):
    half = whole(BOTH, WIDTH // 2)
    return pl.pallas_call(
        second_kernel,
        grid=(RING,),
        out_shape=(bf(BOTH, WIDTH // 2), bf(RING, BOTH + 8, D)),
        in_specs=[half, half] + weight_blocks(D) + [by_group(D, BOTH), whole(1, D)],
        out_specs=(half, by_group(BOTH + 8, D)),
        scratch_shapes=[scratch(1, D, jnp.float32)],
        name="gradients_second",
        interpret=interpret,
    )(mine, other, *weights, attn, square)


def weight_parts(sout, grad_first, grad_second, interpret=False):
    turned = pl.BlockSpec((1, 2, RING, D, D), lambda r: (r, 0, 0, 0, 0))
    return pl.pallas_call(
        weight_kernel,
        grid=(SIDES,),
        out_shape=(bf(SIDES, 2, RING, D, D),) * 2,
        in_specs=[
            whole(RING, BOTH, D),
            pl.BlockSpec((BOTH, COLS * D), lambda r: (0, jnp.minimum(r, CHUNK - 1))),
            pl.BlockSpec((BOTH, COLS * D), lambda r: (0, jnp.maximum(r - CHUNK, 0))),
        ],
        out_specs=(turned, turned),
        scratch_shapes=[pltpu.VMEM((RING, D, BOTH), jnp.bfloat16)],
        name="weight_parts",
        interpret=interpret,
    )(sout, grad_first, grad_second)


def reduce_parts(place, keep, send, run):
    reps = range(GROUPS)
    other = lax.ppermute(send, "rep", [(rep, rep ^ 1) for rep in reps])
    own, *rest = run(add_core_kernel, (bf(2, RING, D, D),) * SIDES, (keep, other))
    moved = []
    for turn, part in enumerate(rest, 1):
        moved.append(
            lax.ppermute(part, "rep", [(rep, (rep - turn * COLS) % GROUPS) for rep in reps])
        )
    own, send = run(add_rows_kernel, (bf(RING, D, D),) * 2, (own, *moved))
    other = lax.ppermute(send, "rep", [(rep, rep ^ 2) for rep in reps])
    own, *rest = run(add_across_kernel, (bf(D, D),) * RING, (place, own, other), scalars=1)
    moved = [lax.ppermute(part, "seq", ring_turn(turn)) for turn, part in enumerate(rest, 1)]
    return run(total_kernel, fl(D, D), (own, *moved))


def tie(value, *after):
    return lax.optimization_barrier((value,) + after)[0]


RINGS = [[ring * RING + place for place in range(RING)] for ring in range(PAIR)]
ACROSS = [(place, (place + RING) % GROUPS) for place in range(GROUPS)]


def gather_columns(student_wo, projection, place, run):
    rep = lax.axis_index("rep")
    reps = range(GROUPS)
    mine = jnp.concatenate(
        [
            lax.dynamic_slice_in_dim(student_wo, rep * D, D, 1),
            lax.dynamic_slice_in_dim(projection, rep * D, D, 1),
        ],
        axis=0,
    )
    pieces = [lax.ppermute(mine, "seq", ring_turn(turn)) for turn in range(1, RING)]
    own = run(gather_kernel, bf(RING, 3 * D, D), (place, mine, *pieces), scalars=1)
    other = lax.ppermute(own, "rep", [(rep, rep ^ 2) for rep in reps])
    rows = [run(join_kernel, bf(2, RING, 3 * D, D), (own, other))]
    for turn in range(1, SIDES):
        rows.append(
            lax.ppermute(rows[0], "rep", [(rep, (rep + turn * COLS) % GROUPS) for rep in reps])
        )
    weights = []
    for part in rows:
        weights += [part, lax.ppermute(part, "rep", [(rep, rep ^ 1) for rep in reps])]
    return weights[:4], weights[4:]


def ring_turn(turn):
    return [(at, at // RING * RING + (at + turn) % RING) for at in range(GROUPS)]


def shards(
    t_query, t_key, t_value, s_query, s_key, student_value, student_wo, projection,
    doc_ids, span_order, interpret=False,
):
    run = functools.partial(call, interpret=interpret)
    order = span_order[0]
    docs = doc_ids[0]
    start = jnp.sum((docs[None, :] < docs[:, None]).astype(jnp.int32), axis=1)
    first = start[::ROWS]
    start = start[:, None]
    place = (lax.axis_index("seq") % RING).reshape(1)

    def swap(blocks):
        return lax.all_to_all(blocks, "seq", split_axis=0, concat_axis=0, tiled=True)

    def swap_ring(blocks):
        return lax.all_to_all(
            blocks, "seq", split_axis=0, concat_axis=0, tiled=True, axis_index_groups=RINGS
        )

    weights = gather_columns(student_wo, projection, place, run)
    s_pack, t_pack = run(
        pack_kernel,
        (bf(GROUPS, TOKENS, 3 * D), bf(GROUPS, TOKENS, 4 * D)),
        (s_query, s_key, student_value, t_query, t_key, t_value),
    )
    s_in = swap(s_pack)
    t_in = swap(tie(t_pack, s_in))
    sout, probs = run(
        student_kernel,
        (bf(RING, BOTH, D), bf(BLOCKS, ROWS, SPAN)),
        (order, first, start, s_in),
        [scratch(LENGTH, D)] + [scratch(LENGTH + LIMIT, D)] * 2 + [scratch(LENGTH, D)],
        scalars=2,
    )
    s_tokens = swap_ring(tie(sout, t_in))
    tout = run(
        teacher_kernel,
        bf(RING, BOTH, 2 * D),
        (order, first, start, t_in),
        [scratch(LENGTH, 2 * D)] + [scratch(LENGTH + LIMIT, D)] * 2 + [scratch(LENGTH, 2 * D)],
        scalars=2,
    )
    t_tokens = swap_ring(tout)
    mine = [terms(s_tokens, t_tokens, half, interpret=interpret) for half in weights]
    other = [lax.ppermute(part, "seq", ACROSS) for part in mine]
    grad_a, attn, square = gradients_first(mine[0], other[0], weights[0], interpret=interpret)
    grad_b, d_attn = gradients_second(
        mine[1], other[1], weights[1], attn, square, interpret=interpret
    )
    grads = swap_ring(d_attn)
    keep, send = weight_parts(s_tokens, grad_a, grad_b, interpret=interpret)
    d_wo = reduce_parts(place, keep, send, run)
    back, loss = run(
        backward_kernel,
        (bf(GROUPS, TOKENS, 3 * D), fl(1, D)),
        (order, first, grads, sout, s_in, probs),
        [scratch(LENGTH, D)] * 3
        + [scratch(LENGTH + LIMIT, D)] * 2
        + [scratch(LENGTH, D)]
        + [scratch(LENGTH + LIMIT, D, jnp.float32)] * 2,
        scalars=2,
    )
    back = swap(back)
    dq, dk, dv = run(
        merge_kernel,
        (bf(TOKENS, GROUPS * D), bf(TOKENS, 4 * D), bf(TOKENS, 4 * D)),
        (back,),
    )
    return loss[0, :1], d_wo, dq[None], dk[None], dv[None]


def solution(mesh):
    tokens = P("rep", "seq", None)
    in_specs = (tokens,) * 6 + (P("seq", None),) * 2 + (P("rep", None),) * 2
    out_specs = (P("rep"), P("seq", "rep"), tokens, tokens, tokens)
    return jax.shard_map(shards, mesh=mesh, in_specs=in_specs, out_specs=out_specs, check_vma=False)
```

```python
import functools
import math

import jax
import jax.numpy as jnp
from jax import lax
from jax.experimental import pallas as pl
from jax.experimental.pallas import tpu as pltpu
from jax.sharding import PartitionSpec as P


D = 128
LENGTH = 2048
HALF = 64
GROUPS = 16
RING = 8
PAIR = GROUPS // RING
TOKENS = LENGTH // GROUPS
WIDTH = 2048
BOTH = PAIR * TOKENS
COLS = 4
BATCH = 4
SIDES = WIDTH // (COLS * D)
CHUNK = WIDTH // (2 * COLS * D)
HALF_COLS = COLS * CHUNK
ROWS = 256
BLOCKS = LENGTH // ROWS
STEP = 128
LIMIT = 512
SPAN = LIMIT + ROWS
SCALE = 1.0 / math.sqrt(D)
LOG2E = math.log2(math.e)
FAR = -1e30


def nt(a, b):
    return lax.dot_general(a, b, (((1,), (1,)), ((), ())), preferred_element_type=jnp.float32)


def nn(a, b):
    return lax.dot_general(a, b, (((1,), (0,)), ((), ())), preferred_element_type=jnp.float32)


def tn(a, b):
    return lax.dot_general(a, b, (((0,), (0,)), ((), ())), preferred_element_type=jnp.float32)


def each_window(first_ref, body, step):
    def one(block, carry):
        needed = (block * ROWS - first_ref[block] + step - 1) // step
        needed = jnp.clip(needed, 0, LIMIT // step)
        for extra in range(LIMIT // step + 1):

            @pl.when(needed == extra)
            def _():
                body(block, ROWS + extra * step)

        return carry

    lax.fori_loop(0, BLOCKS, one, 0)


def stored_slots():
    for group in range(GROUPS):
        for half in range(2):
            yield 2 * group + half, (group, half * HALF)


def ring_slots():
    for group in range(GROUPS):
        for half in range(2):
            yield 2 * group + half, (group % RING, (group // RING) * TOKENS + half * HALF)


def spread(order_ref, src_ref, first, dst, offset, slots):
    cols = slice(first, first + dst.shape[1])
    if offset:
        dst[:offset, :] = jnp.zeros((offset, dst.shape[1]), dst.dtype)
    for slot, (block, row) in slots():
        place = pl.ds(pl.multiple_of(order_ref[slot] * HALF + offset, HALF), HALF)
        dst[place, :] = src_ref[block, row : row + HALF, cols]


def window(start_ref, block, width):
    row = pl.multiple_of(block * ROWS, ROWS)
    keys = pl.ds(pl.multiple_of(row + SPAN - width, STEP), width)
    lane = lax.broadcasted_iota(jnp.int32, (ROWS, width), 1)
    line = lax.broadcasted_iota(jnp.int32, (ROWS, width), 0)
    begin = start_ref[pl.ds(row, ROWS), :] - (row + ROWS - width)
    allowed = (lane >= begin) & (lane - line <= width - ROWS)
    return pl.ds(row, ROWS), keys, jnp.where(allowed, 0.0, FAR)


def weights_of(queries, key_rows, bias):
    scores = nt(queries, key_rows) * (SCALE * LOG2E) + bias
    weights = jnp.exp2(scores - jnp.max(scores, axis=1, keepdims=True))
    return weights, jnp.sum(weights, axis=1, keepdims=True)


def put_back(order_ref, src, out_ref, cols, slots, offset=0, scale=None):
    for slot, (block, row) in slots():
        place = pl.ds(pl.multiple_of(order_ref[slot] * HALF + offset, HALF), HALF)
        value = src[place, :]
        if scale is not None:
            value = (value * scale).astype(out_ref.dtype)
        out_ref[block, row : row + HALF, cols] = value


def teacher_kernel(order_ref, first_ref, start_ref, in_ref, out_ref, tq, tk, tv, to):
    spread(order_ref, in_ref, 0, tq, 0, stored_slots)
    spread(order_ref, in_ref, 2 * D, tk, LIMIT, stored_slots)
    spread(order_ref, in_ref, 3 * D, tv, LIMIT, stored_slots)

    def body(block, width):
        rows, keys, bias = window(start_ref, block, width)
        key_rows = tk[keys, :]
        val_rows = tv[keys, :]
        for head in range(2):
            cols = slice(head * D, (head + 1) * D)
            weights, totals = weights_of(tq[rows, cols], key_rows, bias)
            to[rows, cols] = (nn(weights.astype(jnp.bfloat16), val_rows) / -totals).astype(jnp.bfloat16)

    each_window(first_ref, body, 2 * STEP)
    put_back(order_ref, to, out_ref, slice(0, 2 * D), ring_slots)


def student_kernel(order_ref, first_ref, start_ref, in_ref, out_ref, probs_ref, sq, sk, sv, so):
    spread(order_ref, in_ref, 0, sq, 0, stored_slots)
    spread(order_ref, in_ref, D, sk, LIMIT, stored_slots)
    spread(order_ref, in_ref, 2 * D, sv, LIMIT, stored_slots)

    def body(block, width):
        rows, keys, bias = window(start_ref, block, width)
        weights, totals = weights_of(sq[rows, :], sk[keys, :], bias)
        probs = (weights * (1.0 / totals)).astype(jnp.bfloat16)
        probs_ref[block, :, SPAN - width :] = probs
        so[rows, :] = nn(probs, sv[keys, :]).astype(jnp.bfloat16)

    each_window(first_ref, body, 2 * STEP)
    put_back(order_ref, so, out_ref, slice(0, D), ring_slots)


def backward_kernel(
    order_ref, first_ref, grad_ref, out_ref, in_ref, probs_ref, back_ref, loss_ref,
    go, so, sq, sk, sv, dq, dk, dv,
):
    spread(order_ref, grad_ref, 0, go, 0, ring_slots)
    spread(order_ref, out_ref, 0, so, 0, ring_slots)
    spread(order_ref, in_ref, 0, sq, 0, stored_slots)
    spread(order_ref, in_ref, D, sk, LIMIT, stored_slots)
    spread(order_ref, in_ref, 2 * D, sv, LIMIT, stored_slots)
    squares = grad_ref[:, BOTH : BOTH + 8, :].astype(jnp.float32)
    loss_ref[...] = jnp.broadcast_to(jnp.sum(squares) / (LENGTH * WIDTH), (1, D))
    dk[...] = jnp.zeros_like(dk)
    dv[...] = jnp.zeros_like(dv)

    def body(block, width):
        row = pl.multiple_of(block * ROWS, ROWS)
        rows = pl.ds(row, ROWS)
        keys = pl.ds(pl.multiple_of(row + SPAN - width, STEP), width)
        probs = probs_ref[block, :, SPAN - width :]
        grads = go[rows, :]
        delta = jnp.sum(
            grads.astype(jnp.float32) * so[rows, :].astype(jnp.float32), axis=1, keepdims=True
        )
        d_probs = nt(grads, sv[keys, :])
        d_scores = (probs.astype(jnp.float32) * (d_probs - delta)).astype(jnp.bfloat16)
        dq[rows, :] = (nn(d_scores, sk[keys, :]) * SCALE).astype(jnp.bfloat16)
        dk[keys, :] += tn(d_scores, sq[rows, :])
        dv[keys, :] += tn(probs, grads)

    each_window(first_ref, body, STEP)
    put_back(order_ref, dq, back_ref, slice(0, D), stored_slots)
    put_back(order_ref, dk, back_ref, slice(D, 2 * D), stored_slots, LIMIT, SCALE)
    put_back(order_ref, dv, back_ref, slice(2 * D, 3 * D), stored_slots, LIMIT, 1.0)


def side_by_side(refs, group, rows):
    return jnp.concatenate(
        [ref[side, group, :rows, :] for ref in refs for side in range(2)], axis=1
    )


def terms_kernel(sout_ref, tout_ref, a_ref, b_ref, c_ref, d_ref, part_ref, total):
    @pl.when(pl.program_id(0) == 0)
    def _():
        total[...] = jnp.zeros_like(total)

    def one(group, carry):
        both = jnp.concatenate([sout_ref[group], tout_ref[group]], axis=1)
        term = nn(both, side_by_side((a_ref, b_ref, c_ref, d_ref), group, 3 * D))
        total[...] += term.astype(jnp.bfloat16).astype(jnp.float32)
        return carry

    lax.fori_loop(0, BATCH, one, 0)

    @pl.when(pl.program_id(0) == RING // BATCH - 1)
    def _():
        part_ref[...] = total[...].astype(jnp.bfloat16)


def gradient_once(mine_ref, other_ref, grad_ref, turned, square_ref):
    diff = mine_ref[...].astype(jnp.float32) + other_ref[...].astype(jnp.float32)
    grad = diff.astype(jnp.bfloat16)
    grad_ref[...] = grad
    turned[...] = grad.T
    square = jnp.sum(diff * diff, axis=0, keepdims=True)
    square_ref[...] = sum(square[:, col * D : (col + 1) * D] for col in range(HALF_COLS))


def first_kernel(
    mine_ref, other_ref, a_ref, b_ref, c_ref, d_ref, grad_ref, attn_ref, square_ref, turned
):
    @pl.when(pl.program_id(0) == 0)
    def _():
        gradient_once(mine_ref, other_ref, grad_ref, turned, square_ref)

    def one(group, carry):
        attn_ref[group] = nn(side_by_side((a_ref, b_ref, c_ref, d_ref), group, D), turned[...])
        return carry

    lax.fori_loop(0, BATCH, one, 0)


def second_kernel(
    mine_ref, other_ref, a_ref, b_ref, c_ref, d_ref, attn_in, square_in, grad_ref, attn_ref,
    turned, squares,
):
    @pl.when(pl.program_id(0) == 0)
    def _():
        gradient_once(mine_ref, other_ref, grad_ref, turned, squares)
        squares[...] += square_in[...]

    total = squares[...]
    high = total.astype(jnp.bfloat16).astype(jnp.float32)
    line = lax.broadcasted_iota(jnp.int32, (8, D), 0)
    rows = jnp.where(line == 0, high, jnp.where(line == 1, total - high, 0.0))
    rows = rows.astype(jnp.bfloat16)

    def one(group, carry):
        part = nn(side_by_side((a_ref, b_ref, c_ref, d_ref), group, D), turned[...])
        part += attn_in[group]
        attn_ref[group, :BOTH, :] = part.T.astype(jnp.bfloat16)
        attn_ref[group, BOTH:, :] = rows
        return carry

    lax.fori_loop(0, BATCH, one, 0)


def weight_kernel(sout_ref, first_ref, second_ref, keep_ref, send_ref, turned):
    step = pl.program_id(0)

    @pl.when(step == 0)
    def _():
        for group in range(RING):
            turned[group] = sout_ref[group].T

    grad = jnp.where(step < CHUNK, first_ref[...], second_ref[...])

    def one(pair, carry):
        for half in range(2):
            group = 2 * pair + half
            part = nn(turned[group], grad).astype(jnp.bfloat16)
            for side in range(2):
                keep_ref[0, side, group] = part[:, side * D : (side + 1) * D]
                send_ref[0, side, group] = part[:, (2 + side) * D : (3 + side) * D]
        return carry

    lax.fori_loop(0, RING // 2, one, 0)


def gather_kernel(place_ref, own_ref, *refs):
    out_ref = refs[-1]
    out_ref[place_ref[0]] = own_ref[...]
    for turn, ref in enumerate(refs[:-1], 1):
        out_ref[lax.rem(place_ref[0] - turn + RING, RING)] = ref[...]


def join_kernel(own_ref, other_ref, out_ref):
    def one(group, carry):
        out_ref[0, group] = own_ref[group]
        out_ref[1, group] = other_ref[group]
        return carry

    lax.fori_loop(0, RING, one, 0)


def plus(*values):
    total = values[0].astype(jnp.float32)
    for value in values[1:]:
        total += value.astype(jnp.float32)
    return total.astype(jnp.bfloat16)


def add_core_kernel(keep_ref, other_ref, *out_refs):
    def one(group, carry):
        for turn, out_ref in enumerate(out_refs):
            for side in range(2):
                out_ref[side, group] = plus(
                    keep_ref[turn, side, group], other_ref[turn, side, group]
                )
        return carry

    lax.fori_loop(0, RING, one, 0)


def add_rows_kernel(own_ref, a_ref, b_ref, c_ref, keep_ref, send_ref):
    def one(group, carry):
        for side, out_ref in enumerate((keep_ref, send_ref)):
            out_ref[group] = plus(*(ref[side, group] for ref in (own_ref, a_ref, b_ref, c_ref)))
        return carry

    lax.fori_loop(0, RING, one, 0)


def add_across_kernel(place_ref, own_ref, other_ref, *out_refs):
    for turn, out_ref in enumerate(out_refs):
        group = lax.rem(place_ref[0] + turn, RING)
        out_ref[...] = plus(own_ref[group], other_ref[group])


def total_kernel(*refs):
    total = refs[0][...].astype(jnp.float32)
    for ref in refs[1:-1]:
        total += ref[...].astype(jnp.float32)
    refs[-1][...] = total


def merge_kernel(back_ref, dq_ref, dk_ref, dv_ref):
    share = GROUPS // 4
    for group in range(GROUPS):
        dq_ref[:, group * D : (group + 1) * D] = back_ref[group, :, :D]
    for head in range(4):
        cols = slice(head * D, (head + 1) * D)
        for ref, first in ((dk_ref, D), (dv_ref, 2 * D)):
            summed = back_ref[head * share, :, first : first + D].astype(jnp.float32)
            for other in range(1, share):
                summed += back_ref[head * share + other, :, first : first + D].astype(jnp.float32)
            ref[:, cols] = summed.astype(jnp.bfloat16)


def pack_kernel(sq_ref, sk_ref, sv_ref, tq_ref, tk_ref, tv_ref, s_ref, t_ref):
    share = GROUPS // 4

    def one(head, carry):
        key = pl.ds(pl.multiple_of(head * D, D), D)
        for member in range(share):
            group = head * share + member
            start = pl.multiple_of(group * D, D)
            s_ref[group, :, :D] = sq_ref[0, :, pl.ds(start, D)]
            s_ref[group, :, D : 2 * D] = sk_ref[0, :, key]
            s_ref[group, :, 2 * D :] = sv_ref[0, :, key]
            start = pl.multiple_of(2 * group * D, 2 * D)
            t_ref[group, :, : 2 * D] = tq_ref[0, :, pl.ds(start, 2 * D)]
            t_ref[group, :, 2 * D : 3 * D] = tk_ref[0, :, key]
            t_ref[group, :, 3 * D :] = tv_ref[0, :, key]
        return carry

    lax.fori_loop(0, 4, one, 0)


VM = pl.BlockSpec(memory_space=pltpu.VMEM)
SM = pl.BlockSpec(memory_space=pltpu.SMEM)


def bf(*shape):
    return jax.ShapeDtypeStruct(shape, jnp.bfloat16)


def fl(*shape):
    return jax.ShapeDtypeStruct(shape, jnp.float32)


def scratch(rows, cols, dtype=jnp.bfloat16):
    return pltpu.VMEM((rows, cols), dtype)


def call(kernel, outs, ins, scratches=(), scalars=0, interpret=False):
    specs = [SM] * scalars + [VM] * (len(ins) - scalars)
    single = not isinstance(outs, tuple)
    return pl.pallas_call(
        kernel,
        out_shape=outs,
        in_specs=specs,
        out_specs=VM if single else (VM,) * len(outs),
        scratch_shapes=list(scratches),
        interpret=interpret,
    )(*ins)


def whole(*shape):
    return pl.BlockSpec(shape, lambda r: (0,) * len(shape))


def by_group(*shape):
    return pl.BlockSpec((BATCH,) + shape, lambda g: (g,) + (0,) * len(shape))


def weight_blocks(rows):
    return [pl.BlockSpec((2, BATCH, rows, D), lambda g: (0, g, 0, 0))] * 4


def terms(sout, tout, weights, interpret=False):
    return pl.pallas_call(
        terms_kernel,
        grid=(RING // BATCH,),
        out_shape=bf(BOTH, WIDTH // 2),
        in_specs=[by_group(BOTH, D), by_group(BOTH, 2 * D)] + weight_blocks(3 * D),
        out_specs=whole(BOTH, WIDTH // 2),
        scratch_shapes=[scratch(BOTH, WIDTH // 2, jnp.float32)],
        name="terms",
        interpret=interpret,
    )(sout, tout, *weights)


def gradients_first(mine, other, weights, interpret=False):
    half = whole(BOTH, WIDTH // 2)
    return pl.pallas_call(
        first_kernel,
        grid=(RING // BATCH,),
        out_shape=(bf(BOTH, WIDTH // 2), fl(RING, D, BOTH), fl(1, D)),
        in_specs=[half, half] + weight_blocks(D),
        out_specs=(half, by_group(D, BOTH), whole(1, D)),
        scratch_shapes=[scratch(WIDTH // 2, BOTH)],
        name="gradients_first",
        interpret=interpret,
    )(mine, other, *weights)


def gradients_second(mine, other, weights, attn, square, interpret=False):
    half = whole(BOTH, WIDTH // 2)
    return pl.pallas_call(
        second_kernel,
        grid=(RING // BATCH,),
        out_shape=(bf(BOTH, WIDTH // 2), bf(RING, BOTH + 8, D)),
        in_specs=[half, half] + weight_blocks(D) + [by_group(D, BOTH), whole(1, D)],
        out_specs=(half, by_group(BOTH + 8, D)),
        scratch_shapes=[scratch(WIDTH // 2, BOTH), scratch(1, D, jnp.float32)],
        name="gradients_second",
        interpret=interpret,
    )(mine, other, *weights, attn, square)


def weight_parts(sout, grad_first, grad_second, interpret=False):
    turned = pl.BlockSpec((1, 2, RING, D, D), lambda r: (r, 0, 0, 0, 0))
    return pl.pallas_call(
        weight_kernel,
        grid=(SIDES,),
        out_shape=(bf(SIDES, 2, RING, D, D),) * 2,
        in_specs=[
            whole(RING, BOTH, D),
            pl.BlockSpec((BOTH, COLS * D), lambda r: (0, jnp.minimum(r, CHUNK - 1))),
            pl.BlockSpec((BOTH, COLS * D), lambda r: (0, jnp.maximum(r - CHUNK, 0))),
        ],
        out_specs=(turned, turned),
        scratch_shapes=[pltpu.VMEM((RING, D, BOTH), jnp.bfloat16)],
        name="weight_parts",
        interpret=interpret,
    )(sout, grad_first, grad_second)


def reduce_parts(place, keep, send, run):
    reps = range(GROUPS)
    other = lax.ppermute(send, "rep", [(rep, rep ^ 1) for rep in reps])
    own, *rest = run(add_core_kernel, (bf(2, RING, D, D),) * SIDES, (keep, other))
    moved = []
    for turn, part in enumerate(rest, 1):
        moved.append(
            lax.ppermute(part, "rep", [(rep, (rep - turn * COLS) % GROUPS) for rep in reps])
        )
    own, send = run(add_rows_kernel, (bf(RING, D, D),) * 2, (own, *moved))
    other = lax.ppermute(send, "rep", [(rep, rep ^ 2) for rep in reps])
    own, *rest = run(add_across_kernel, (bf(D, D),) * RING, (place, own, other), scalars=1)
    moved = [lax.ppermute(part, "seq", ring_turn(turn)) for turn, part in enumerate(rest, 1)]
    return run(total_kernel, fl(D, D), (own, *moved))


def tie(value, *after):
    return lax.optimization_barrier((value,) + after)[0]


RINGS = [[ring * RING + place for place in range(RING)] for ring in range(PAIR)]
ACROSS = [(place, (place + RING) % GROUPS) for place in range(GROUPS)]


def gather_columns(student_wo, projection, place, run):
    rep = lax.axis_index("rep")
    reps = range(GROUPS)
    mine = jnp.concatenate(
        [
            lax.dynamic_slice_in_dim(student_wo, rep * D, D, 1),
            lax.dynamic_slice_in_dim(projection, rep * D, D, 1),
        ],
        axis=0,
    )
    pieces = [lax.ppermute(mine, "seq", ring_turn(turn)) for turn in range(1, RING)]
    own = run(gather_kernel, bf(RING, 3 * D, D), (place, mine, *pieces), scalars=1)
    other = lax.ppermute(own, "rep", [(rep, rep ^ 2) for rep in reps])
    rows = [run(join_kernel, bf(2, RING, 3 * D, D), (own, other))]
    for turn in range(1, SIDES):
        rows.append(
            lax.ppermute(rows[0], "rep", [(rep, (rep + turn * COLS) % GROUPS) for rep in reps])
        )
    weights = []
    for part in rows:
        weights += [part, lax.ppermute(part, "rep", [(rep, rep ^ 1) for rep in reps])]
    return weights[:4], weights[4:]


def ring_turn(turn):
    return [(at, at // RING * RING + (at + turn) % RING) for at in range(GROUPS)]


def shards(
    t_query, t_key, t_value, s_query, s_key, student_value, student_wo, projection,
    doc_ids, span_order, interpret=False,
):
    run = functools.partial(call, interpret=interpret)
    order = span_order[0]
    docs = doc_ids[0]
    start = jnp.sum((docs[None, :] < docs[:, None]).astype(jnp.int32), axis=1)
    first = start[::ROWS]
    start = start[:, None]
    place = (lax.axis_index("seq") % RING).reshape(1)

    def swap(blocks):
        return lax.all_to_all(blocks, "seq", split_axis=0, concat_axis=0, tiled=True)

    def swap_ring(blocks):
        return lax.all_to_all(
            blocks, "seq", split_axis=0, concat_axis=0, tiled=True, axis_index_groups=RINGS
        )

    weights = gather_columns(student_wo, projection, place, run)
    s_pack, t_pack = run(
        pack_kernel,
        (bf(GROUPS, TOKENS, 3 * D), bf(GROUPS, TOKENS, 4 * D)),
        (s_query, s_key, student_value, t_query, t_key, t_value),
    )
    s_in = swap(s_pack)
    t_in = swap(tie(t_pack, s_in))
    sout, probs = run(
        student_kernel,
        (bf(RING, BOTH, D), bf(BLOCKS, ROWS, SPAN)),
        (order, first, start, s_in),
        [scratch(LENGTH, D)] + [scratch(LENGTH + LIMIT, D)] * 2 + [scratch(LENGTH, D)],
        scalars=2,
    )
    s_tokens = swap_ring(tie(sout, t_in))
    tout = run(
        teacher_kernel,
        bf(RING, BOTH, 2 * D),
        (order, first, start, t_in),
        [scratch(LENGTH, 2 * D)] + [scratch(LENGTH + LIMIT, D)] * 2 + [scratch(LENGTH, 2 * D)],
        scalars=2,
    )
    t_tokens = swap_ring(tout)
    mine = [terms(s_tokens, t_tokens, half, interpret=interpret) for half in weights]
    other = [lax.ppermute(part, "seq", ACROSS) for part in mine]
    grad_a, attn, square = gradients_first(mine[0], other[0], weights[0], interpret=interpret)
    grad_b, d_attn = gradients_second(
        mine[1], other[1], weights[1], attn, square, interpret=interpret
    )
    grads = swap_ring(d_attn)
    keep, send = weight_parts(s_tokens, grad_a, grad_b, interpret=interpret)
    d_wo = reduce_parts(place, keep, send, run)
    back, loss = run(
        backward_kernel,
        (bf(GROUPS, TOKENS, 3 * D), fl(1, D)),
        (order, first, grads, sout, s_in, probs),
        [scratch(LENGTH, D)] * 3
        + [scratch(LENGTH + LIMIT, D)] * 2
        + [scratch(LENGTH, D)]
        + [scratch(LENGTH + LIMIT, D, jnp.float32)] * 2,
        scalars=2,
    )
    back = swap(back)
    dq, dk, dv = run(
        merge_kernel,
        (bf(TOKENS, GROUPS * D), bf(TOKENS, 4 * D), bf(TOKENS, 4 * D)),
        (back,),
    )
    return loss[0, :1], d_wo, dq[None], dk[None], dv[None]


def solution(mesh):
    tokens = P("rep", "seq", None)
    in_specs = (tokens,) * 6 + (P("seq", None),) * 2 + (P("rep", None),) * 2
    out_specs = (P("rep"), P("seq", "rep"), tokens, tokens, tokens)
    return jax.shard_map(shards, mesh=mesh, in_specs=in_specs, out_specs=out_specs, check_vma=False)
```

```python
import functools
import math

import jax
import jax.numpy as jnp
from jax import lax
from jax.experimental import pallas as pl
from jax.experimental.pallas import tpu as pltpu
from jax.sharding import PartitionSpec as P


D = 128
LENGTH = 2048
HALF = 64
GROUPS = 16
RING = 8
PAIR = GROUPS // RING
TOKENS = LENGTH // GROUPS
WIDTH = 2048
BOTH = PAIR * TOKENS
COLS = 4
PADDED = 528
SIDES = WIDTH // (COLS * D)
CHUNK = WIDTH // (2 * COLS * D)
ROWS = 256
BLOCKS = LENGTH // ROWS
STEP = 128
LIMIT = 512
SPAN = LIMIT + ROWS
STEPS = LIMIT // STEP + 1
SCALE = 1.0 / math.sqrt(D)
LOG2E = math.log2(math.e)
FAR = -1e30


def nt(a, b):
    return lax.dot_general(a, b, (((1,), (1,)), ((), ())), preferred_element_type=jnp.float32)


def nn(a, b):
    return lax.dot_general(a, b, (((1,), (0,)), ((), ())), preferred_element_type=jnp.float32)


def tn(a, b):
    return lax.dot_general(a, b, (((0,), (0,)), ((), ())), preferred_element_type=jnp.float32)


def key_steps(first_ref, block):
    return jnp.clip((block * ROWS - first_ref[block] + STEP - 1) // STEP, 0, STEPS - 1)


def each_window(first_ref, body):
    def one(block, carry):
        needed = key_steps(first_ref, block)
        for extra in range(STEPS):
            width = ROWS + extra * STEP

            @pl.when(needed == extra)
            def _():
                body(block, width)

        return carry

    lax.fori_loop(0, BLOCKS, one, 0)


def stored_slots():
    for group in range(GROUPS):
        for half in range(2):
            yield 2 * group + half, (group, half * HALF)


def ring_slots():
    for group in range(GROUPS):
        for half in range(2):
            yield 2 * group + half, (group % RING, (group // RING) * TOKENS + half * HALF)


def spread(order_ref, src_ref, first, dst, offset, slots):
    cols = slice(first, first + dst.shape[1])
    if offset:
        dst[:offset, :] = jnp.zeros((offset, dst.shape[1]), dst.dtype)
    for slot, (block, row) in slots():
        place = pl.ds(pl.multiple_of(order_ref[slot] * HALF + offset, HALF), HALF)
        dst[place, :] = src_ref[block, row : row + HALF, cols]


def window(start_ref, block, width):
    row = pl.multiple_of(block * ROWS, ROWS)
    keys = pl.ds(pl.multiple_of(row + SPAN - width, STEP), width)
    lane = lax.broadcasted_iota(jnp.int32, (ROWS, width), 1)
    line = lax.broadcasted_iota(jnp.int32, (ROWS, width), 0)
    begin = start_ref[pl.ds(row, ROWS), :] - (row + ROWS - width)
    allowed = (lane >= begin) & (lane - line <= width - ROWS)
    return pl.ds(row, ROWS), keys, jnp.where(allowed, 0.0, FAR)


def weights_of(queries, key_rows, bias):
    scores = nt(queries, key_rows) * (SCALE * LOG2E) + bias
    weights = jnp.exp2(scores - jnp.max(scores, axis=1, keepdims=True))
    return weights, jnp.sum(weights, axis=1, keepdims=True)


def put_back(order_ref, src, out_ref, cols, slots, offset=0, scale=None):
    for slot, (block, row) in slots():
        place = pl.ds(pl.multiple_of(order_ref[slot] * HALF + offset, HALF), HALF)
        value = src[place, :]
        if scale is not None:
            value = (value * scale).astype(out_ref.dtype)
        out_ref[block, row : row + HALF, cols] = value


def teacher_kernel(order_ref, first_ref, start_ref, in_ref, out_ref, tq, tk, tv, to):
    spread(order_ref, in_ref, 0, tq, 0, stored_slots)
    spread(order_ref, in_ref, 2 * D, tk, LIMIT, stored_slots)
    spread(order_ref, in_ref, 3 * D, tv, LIMIT, stored_slots)

    def body(block, width):
        rows, keys, bias = window(start_ref, block, width)
        key_rows = tk[keys, :]
        val_rows = tv[keys, :]
        for head in range(2):
            cols = slice(head * D, (head + 1) * D)
            weights, totals = weights_of(tq[rows, cols], key_rows, bias)
            to[rows, cols] = (nn(weights.astype(jnp.bfloat16), val_rows) / -totals).astype(jnp.bfloat16)

    each_window(first_ref, body)
    put_back(order_ref, to, out_ref, slice(0, 2 * D), ring_slots)


def student_kernel(order_ref, first_ref, start_ref, in_ref, out_ref, probs_ref, sq, sk, sv, so):
    spread(order_ref, in_ref, 0, sq, 0, stored_slots)
    spread(order_ref, in_ref, D, sk, LIMIT, stored_slots)
    spread(order_ref, in_ref, 2 * D, sv, LIMIT, stored_slots)

    def body(block, width):
        rows, keys, bias = window(start_ref, block, width)
        weights, totals = weights_of(sq[rows, :], sk[keys, :], bias)
        probs = (weights * (1.0 / totals)).astype(jnp.bfloat16)
        probs_ref[block, :, SPAN - width :] = probs
        so[rows, :] = nn(probs, sv[keys, :]).astype(jnp.bfloat16)

    each_window(first_ref, body)
    put_back(order_ref, so, out_ref, slice(0, D), ring_slots)


def backward_kernel(
    order_ref, first_ref, grad_ref, out_ref, in_ref, probs_ref, back_ref, loss_ref,
    go, so, sq, sk, sv, dq, dk, dv,
):
    spread(order_ref, grad_ref, 0, go, 0, ring_slots)
    spread(order_ref, out_ref, 0, so, 0, ring_slots)
    spread(order_ref, in_ref, 0, sq, 0, stored_slots)
    spread(order_ref, in_ref, D, sk, LIMIT, stored_slots)
    spread(order_ref, in_ref, 2 * D, sv, LIMIT, stored_slots)
    squares = grad_ref[:, BOTH : BOTH + 8, :].astype(jnp.float32)
    loss_ref[...] = jnp.broadcast_to(jnp.sum(squares) / (LENGTH * WIDTH), (1, D))
    dk[...] = jnp.zeros_like(dk)
    dv[...] = jnp.zeros_like(dv)

    def body(block, width):
        row = pl.multiple_of(block * ROWS, ROWS)
        rows = pl.ds(row, ROWS)
        keys = pl.ds(pl.multiple_of(row + SPAN - width, STEP), width)
        probs = probs_ref[block, :, SPAN - width :]
        grads = go[rows, :]
        delta = jnp.sum(
            grads.astype(jnp.float32) * so[rows, :].astype(jnp.float32), axis=1, keepdims=True
        )
        d_probs = nt(grads, sv[keys, :])
        d_scores = (probs.astype(jnp.float32) * (d_probs - delta)).astype(jnp.bfloat16)
        dq[rows, :] = (nn(d_scores, sk[keys, :]) * SCALE).astype(jnp.bfloat16)
        dk[keys, :] += tn(d_scores, sq[rows, :])
        dv[keys, :] += tn(probs, grads)

    each_window(first_ref, body)
    put_back(order_ref, dq, back_ref, slice(0, D), stored_slots)
    put_back(order_ref, dk, back_ref, slice(D, 2 * D), stored_slots, LIMIT, SCALE)
    put_back(order_ref, dv, back_ref, slice(2 * D, 3 * D), stored_slots, LIMIT, 1.0)


def side_by_side(w_ref, group, rows):
    return jnp.concatenate([w_ref[col, group, :rows, :] for col in range(COLS)], axis=1)


def terms_kernel(sout_ref, tout_ref, w_ref, part_ref):
    total = None
    for group in range(RING):
        both = jnp.concatenate([sout_ref[group], tout_ref[group]], axis=1)
        term = nn(both, side_by_side(w_ref, group, 3 * D))
        term = term.astype(jnp.bfloat16).astype(jnp.float32)
        total = term if total is None else total + term
    part_ref[...] = total.astype(jnp.bfloat16)


def gradient_step(mine_ref, other_ref, w_ref, grad_ref):
    diff = mine_ref[...].astype(jnp.float32) + other_ref[...].astype(jnp.float32)
    grad = diff.astype(jnp.bfloat16)
    grad_ref[...] = grad
    square = jnp.sum(diff * diff, axis=0, keepdims=True)
    square = sum(square[:, col * D : (col + 1) * D] for col in range(COLS))
    wo = jnp.concatenate([side_by_side(w_ref, group, D) for group in range(RING)], axis=0)
    return nt(wo, grad), square


def first_kernel(mine_ref, other_ref, w_ref, grad_ref, attn_ref, square_ref):
    part, square = gradient_step(mine_ref, other_ref, w_ref, grad_ref)

    @pl.when(pl.program_id(0) == 0)
    def _():
        attn_ref[...] = part
        square_ref[...] = square

    @pl.when(pl.program_id(0) > 0)
    def _():
        attn_ref[...] += part
        square_ref[...] += square


def second_kernel(mine_ref, other_ref, w_ref, attn_in, square_in, grad_ref, attn_ref, attn, squares):
    part, square = gradient_step(mine_ref, other_ref, w_ref, grad_ref)
    step = pl.program_id(0)

    @pl.when(step == 0)
    def _():
        attn[...] = attn_in[...] + part
        squares[...] = square_in[...] + square

    @pl.when(step > 0)
    def _():
        attn[...] += part
        squares[...] += square

    @pl.when(step == pl.num_programs(0) - 1)
    def _():
        for group in range(RING):
            block = attn[group * D : (group + 1) * D, :]
            attn_ref[group, :BOTH, :] = block.T.astype(jnp.bfloat16)
        total = squares[...]
        high = total.astype(jnp.bfloat16).astype(jnp.float32)
        line = lax.broadcasted_iota(jnp.int32, (8, D), 0)
        rows = jnp.where(line == 0, high, jnp.where(line == 1, total - high, 0.0))
        for group in range(RING):
            attn_ref[group, BOTH:, :] = rows.astype(jnp.bfloat16)


def weight_kernel(away, place_ref, sout_ref, first_ref, second_ref, part_ref, turned):
    step = pl.program_id(0)

    @pl.when(step == 0)
    def _():
        for group in range(RING):
            turned[group] = sout_ref[group].T

    grad = jnp.where(step < CHUNK, first_ref[...], second_ref[...])
    high = jnp.bitwise_xor(place_ref[2], away) == 1
    cols = jnp.concatenate(
        [
            jnp.where(high, grad[:, (side + 1) * D : (side + 2) * D], grad[:, side * D : (side + 1) * D])
            for side in (0, 2)
        ],
        axis=1,
    )
    for group in range(RING):
        part = nn(turned[group], cols).astype(jnp.bfloat16)
        for side in range(2):
            across = jnp.bitwise_xor(place_ref[1], side)
            part_ref[0, across, group] = part[:, side * D : (side + 1) * D]


def plus(*values):
    total = values[0].astype(jnp.float32)
    for value in values[1:]:
        total += value.astype(jnp.float32)
    return total.astype(jnp.bfloat16)


ADD = 4


def add_core_kernel(keep_ref, other_ref, *out_refs):
    def one(group, carry):
        for turn, out_ref in enumerate(out_refs):
            for side in range(2):
                out_ref[side, group] = plus(
                    keep_ref[turn, side, group], other_ref[turn, side, group]
                )
        return carry

    lax.fori_loop(0, ADD, one, 0)


def add_rows_kernel(own_ref, a_ref, b_ref, c_ref, keep_ref, send_ref):
    def one(group, carry):
        for side, out_ref in enumerate((keep_ref, send_ref)):
            out_ref[group] = plus(*(ref[side, group] for ref in (own_ref, a_ref, b_ref, c_ref)))
        return carry

    lax.fori_loop(0, RING, one, 0)


def add_across_kernel(place_ref, own_ref, other_ref, *out_refs):
    for turn, out_ref in enumerate(out_refs):
        group = lax.rem(place_ref[3] + turn, RING)
        out_ref[...] = plus(own_ref[group], other_ref[group])


def total_kernel(*refs):
    total = refs[0][...].astype(jnp.float32)
    for ref in refs[1:-1]:
        total += ref[...].astype(jnp.float32)
    refs[-1][...] = total


def merge_kernel(back_ref, dq_ref, dk_ref, dv_ref):
    share = GROUPS // 4
    for group in range(GROUPS):
        dq_ref[:, group * D : (group + 1) * D] = back_ref[group, :, :D]
    for head in range(4):
        cols = slice(head * D, (head + 1) * D)
        for ref, first in ((dk_ref, D), (dv_ref, 2 * D)):
            summed = back_ref[head * share, :, first : first + D].astype(jnp.float32)
            for other in range(1, share):
                summed += back_ref[head * share + other, :, first : first + D].astype(jnp.float32)
            ref[:, cols] = summed.astype(jnp.bfloat16)


def pack_kernel(sq_ref, sk_ref, sv_ref, tq_ref, tk_ref, tv_ref, s_ref, t_ref):
    share = GROUPS // 4
    for group in range(GROUPS):
        key = slice((group // share) * D, (group // share + 1) * D)
        s_ref[group, :, :D] = sq_ref[0, :, group * D : (group + 1) * D]
        s_ref[group, :, D : 2 * D] = sk_ref[0, :, key]
        s_ref[group, :, 2 * D :] = sv_ref[0, :, key]
        t_ref[group, :, : 2 * D] = tq_ref[0, :, 2 * group * D : 2 * (group + 1) * D]
        t_ref[group, :, 2 * D : 3 * D] = tk_ref[0, :, key]
        t_ref[group, :, 3 * D :] = tv_ref[0, :, key]


VM = pl.BlockSpec(memory_space=pltpu.VMEM)
SM = pl.BlockSpec(memory_space=pltpu.SMEM)


def bf(*shape):
    return jax.ShapeDtypeStruct(shape, jnp.bfloat16)


def fl(*shape):
    return jax.ShapeDtypeStruct(shape, jnp.float32)


def scratch(rows, cols, dtype=jnp.bfloat16):
    return pltpu.VMEM((rows, cols), dtype)


def call(kernel, outs, ins, scratches=(), scalars=0, interpret=False):
    specs = [SM] * scalars + [VM] * (len(ins) - scalars)
    single = not isinstance(outs, tuple)
    return pl.pallas_call(
        kernel,
        out_shape=outs,
        in_specs=specs,
        out_specs=VM if single else (VM,) * len(outs),
        scratch_shapes=list(scratches),
        interpret=interpret,
    )(*ins)


def whole(*shape):
    return pl.BlockSpec(shape, lambda r: (0,) * len(shape))


def by_columns(rows):
    return pl.BlockSpec((rows, COLS * D), lambda r: (0, r))


def weight_block(rows, half):
    return pl.BlockSpec((COLS, RING, rows, D), lambda r: (r + half * CHUNK, 0, 0, 0))


def terms(sout, tout, weights, half, interpret=False):
    return pl.pallas_call(
        terms_kernel,
        grid=(CHUNK,),
        out_shape=bf(BOTH, WIDTH // 2),
        in_specs=[whole(RING, BOTH, D), whole(RING, BOTH, 2 * D), weight_block(3 * D, half)],
        out_specs=by_columns(BOTH),
        name="terms",
        interpret=interpret,
    )(sout, tout, weights)


def gradients_first(mine, other, weights, interpret=False):
    return pl.pallas_call(
        first_kernel,
        grid=(CHUNK,),
        out_shape=(bf(BOTH, WIDTH // 2), fl(RING * D, BOTH), fl(1, D)),
        in_specs=[by_columns(BOTH), by_columns(BOTH), weight_block(D, 0)],
        out_specs=(by_columns(BOTH), whole(RING * D, BOTH), whole(1, D)),
        name="gradients_first",
        interpret=interpret,
    )(mine, other, weights)


def gradients_second(mine, other, weights, attn, square, interpret=False):
    return pl.pallas_call(
        second_kernel,
        grid=(CHUNK,),
        out_shape=(bf(BOTH, WIDTH // 2), bf(RING, BOTH + 8, D)),
        in_specs=[
            by_columns(BOTH), by_columns(BOTH), weight_block(D, 1),
            whole(RING * D, BOTH), whole(1, D),
        ],
        out_specs=(by_columns(BOTH), whole(RING, BOTH + 8, D)),
        scratch_shapes=[scratch(RING * D, BOTH, jnp.float32), scratch(1, D, jnp.float32)],
        name="gradients_second",
        interpret=interpret,
    )(mine, other, weights, attn, square)


def weight_parts(place, sout, grad_first, grad_second, away, interpret=False):
    turned = pl.BlockSpec(
        (1, 2, RING, D, D), lambda r, at: (lax.rem(r - at[0] + SIDES, SIDES), 0, 0, 0, 0)
    )
    return pl.pallas_call(
        functools.partial(weight_kernel, away),
        grid_spec=pltpu.PrefetchScalarGridSpec(
            num_scalar_prefetch=1,
            grid=(SIDES,),
            in_specs=[
                pl.BlockSpec((RING, BOTH, D), lambda r, at: (0, 0, 0)),
                pl.BlockSpec((BOTH, COLS * D), lambda r, at: (0, jnp.minimum(r, CHUNK - 1))),
                pl.BlockSpec((BOTH, COLS * D), lambda r, at: (0, jnp.maximum(r - CHUNK, 0))),
            ],
            out_specs=turned,
            scratch_shapes=[pltpu.VMEM((RING, D, BOTH), jnp.bfloat16)],
        ),
        out_shape=bf(SIDES, 2, RING, D, D),
        name="weight_parts",
        interpret=interpret,
    )(place, sout, grad_first, grad_second)


def add_core(keep, other, interpret=False):
    taken = pl.BlockSpec((SIDES, 2, ADD, D, D), lambda r: (0, 0, r, 0, 0))
    given = pl.BlockSpec((2, ADD, D, D), lambda r: (0, r, 0, 0))
    return pl.pallas_call(
        add_core_kernel,
        grid=(RING // ADD,),
        out_shape=(bf(2, RING, D, D),) * SIDES,
        in_specs=[taken, taken],
        out_specs=(given,) * SIDES,
        name="add_core_kernel",
        interpret=interpret,
    )(keep, other)


def reduce_parts(place, keep, other, run):
    reps = range(GROUPS)
    own, *rest = add_core(keep, other, **run.keywords)
    moved = []
    for turn, part in enumerate(rest, 1):
        moved.append(
            lax.ppermute(part, "rep", [(rep, (rep + turn * COLS) % GROUPS) for rep in reps])
        )
    own, send = run(add_rows_kernel, (bf(RING, D, D),) * 2, (own, *moved))
    other = lax.ppermute(send, "rep", [(rep, rep ^ 2) for rep in reps])
    own, *rest = run(add_across_kernel, (bf(D, D),) * RING, (place, own, other), scalars=1)
    moved = [
        lax.ppermute(
            part,
            "seq",
            [(at, at // RING * RING + (at + turn) % RING) for at in range(GROUPS)],
        )
        for turn, part in enumerate(rest, 1)
    ]
    return run(total_kernel, fl(D, D), (own, *moved))


def tie(value, *after):
    return lax.optimization_barrier((value,) + after)[0]


RINGS = [[ring * RING + place for place in range(RING)] for ring in range(PAIR)]
ACROSS = [(place, (place + RING) % GROUPS) for place in range(GROUPS)]


def unpad_kernel(in_ref, out_ref):
    for place in range(RING):
        out_ref[place * 3 * D : (place + 1) * 3 * D, :] = in_ref[place, : 3 * D, :]


def gather_columns(student_wo, projection, run):
    rep = lax.axis_index("rep")
    mine = jnp.concatenate(
        [
            lax.dynamic_slice_in_dim(student_wo, rep * D, D, 1),
            lax.dynamic_slice_in_dim(projection, rep * D, D, 1),
            jnp.zeros((PADDED - 3 * D, D), jnp.bfloat16),
        ],
        axis=0,
    )
    pieces = lax.all_gather(mine, "seq", axis=0, axis_index_groups=RINGS)
    pieces = run(unpad_kernel, bf(RING * 3 * D, D), (pieces,))
    columns = lax.all_gather(pieces, "rep", axis=0)
    return columns.reshape(-1, RING, 3 * D, D)


def shards(
    t_query, t_key, t_value, s_query, s_key, student_value, student_wo, projection,
    doc_ids, span_order, interpret=False,
):
    run = functools.partial(call, interpret=interpret)
    order = span_order[0]
    docs = doc_ids[0]
    start = jnp.sum((docs[None, :] < docs[:, None]).astype(jnp.int32), axis=1)
    first = start[::ROWS]
    start = start[:, None]
    rep = lax.axis_index("rep")
    place = jnp.stack([rep // 4, (rep // 2) % 2, rep % 2, lax.axis_index("seq") % RING])

    def swap(blocks):
        return lax.all_to_all(blocks, "seq", split_axis=0, concat_axis=0, tiled=True)

    def swap_ring(blocks):
        return lax.all_to_all(
            blocks, "seq", split_axis=0, concat_axis=0, tiled=True, axis_index_groups=RINGS
        )

    weights = gather_columns(student_wo, projection, run)
    s_pack, t_pack = run(
        pack_kernel,
        (bf(GROUPS, TOKENS, 3 * D), bf(GROUPS, TOKENS, 4 * D)),
        (s_query, s_key, student_value, t_query, t_key, t_value),
    )
    s_in = swap(s_pack)
    t_in = swap(tie(t_pack, s_in))
    sout, probs = run(
        student_kernel,
        (bf(RING, BOTH, D), bf(BLOCKS, ROWS, SPAN)),
        (order, first, start, s_in),
        [scratch(LENGTH, D)] + [scratch(LENGTH + LIMIT, D)] * 2 + [scratch(LENGTH, D)],
        scalars=2,
    )
    s_tokens = swap_ring(tie(sout, t_in))
    tout = run(
        teacher_kernel,
        bf(RING, BOTH, 2 * D),
        (order, first, start, t_in),
        [scratch(LENGTH, 2 * D)] + [scratch(LENGTH + LIMIT, D)] * 2 + [scratch(LENGTH, 2 * D)],
        scalars=2,
    )
    t_tokens = swap_ring(tout)
    mine = [terms(s_tokens, t_tokens, weights, half, interpret=interpret) for half in range(2)]
    other = [lax.ppermute(part, "seq", ACROSS) for part in mine]
    grad_a, attn, square = gradients_first(mine[0], other[0], weights, interpret=interpret)
    grad_b, d_attn = gradients_second(
        mine[1], other[1], weights, attn, square, interpret=interpret
    )
    grads = swap_ring(d_attn)
    away = weight_parts(place, s_tokens, grad_a, grad_b, 1, interpret=interpret)
    other = lax.ppermute(away, "rep", [(rep, rep ^ 1) for rep in range(GROUPS)])
    keep = weight_parts(place, s_tokens, grad_a, grad_b, 0, interpret=interpret)
    d_wo = reduce_parts(place, keep, other, run)
    back, loss = run(
        backward_kernel,
        (bf(GROUPS, TOKENS, 3 * D), fl(1, D)),
        (order, first, grads, sout, s_in, probs),
        [scratch(LENGTH, D)] * 3
        + [scratch(LENGTH + LIMIT, D)] * 2
        + [scratch(LENGTH, D)]
        + [scratch(LENGTH + LIMIT, D, jnp.float32)] * 2,
        scalars=2,
    )
    back = swap(back)
    dq, dk, dv = run(
        merge_kernel,
        (bf(TOKENS, GROUPS * D), bf(TOKENS, 4 * D), bf(TOKENS, 4 * D)),
        (back,),
    )
    return loss[0, :1], d_wo, dq[None], dk[None], dv[None]


def solution(mesh):
    tokens = P("rep", "seq", None)
    in_specs = (tokens,) * 6 + (P("seq", None),) * 2 + (P("rep", None),) * 2
    out_specs = (P("rep"), P("seq", "rep"), tokens, tokens, tokens)
    return jax.shard_map(shards, mesh=mesh, in_specs=in_specs, out_specs=out_specs, check_vma=False)
```
